256 devices in a mesh: gx: 8 (over x, y_hi), gy: 4 (over y_lo, core), gz: 8 (over z).
Axes of the slice: x: 4, y: 4 (y_hi: 2, y_lo: 2; y = y_hi * 2 + y_lo), z: 8, core: 2. Of those that a mesh axis runs over, the one named last changes fastest.
Arguments:
- features: bfloat16 [32, 32, 256, 1024], P(None, 'gx', 'gy', 'gz'), may hold values from -6 to 6
- conv_weight: bfloat16 [27, 32], replicated, may hold values from -0.21875 to 0.21875
- mask: int32 [32, 256, 1024], P('gx', 'gy', 'gz'), may hold values from 0 to 1, as said below
Outputs:
- score: float32 [32, 256, 1024], P('gx', 'gy', 'gz')
- depth: float32 [32, 256, 1024], P('gx', 'gy', 'gz')
The draws below stay inside these ranges and needn't reach their ends.
Inputs may be any that keep to these rules, and one draw needn't show every extreme that they name: `mask`: 1 marks a foreground voxel and 0 a background voxel; every draw holds both.
All inputs are finite; a program needn't handle non-finite values.
Results may differ from the reference program's by a relative error of at most 0.0003.
Values may be sent and summed in bfloat16 or wider, within the bound.
A program may use at most 128 MiB of HBM per device.

```python
import jax
import jax.numpy as jnp
from jax import lax

CH = 32
RADIUS = 128
NX = 32
NY = 256
NZ = 1024


def draw_mask(key, part):
    count = max(2, NX * NY * NZ // (2 * RADIUS ** 3))
    centre_x = jax.random.randint(jax.random.fold_in(key, 11), (count,), 0, NX, dtype=jnp.int32)
    centre_y = jax.random.randint(jax.random.fold_in(key, 12), (count,), 0, NY, dtype=jnp.int32)
    centre_z = jax.random.randint(jax.random.fold_in(key, 13), (count,), 0, NZ, dtype=jnp.int32)
    radius_all = jax.random.randint(jax.random.fold_in(key, 14), (count,), RADIUS // 2, 3 * RADIUS // 2, dtype=jnp.int32)
    empty_x = jax.random.randint(jax.random.fold_in(key, 15), (), 0, NX, dtype=jnp.int32)
    empty_y = jax.random.randint(jax.random.fold_in(key, 16), (), 0, NY, dtype=jnp.int32)
    empty_z = (centre_z[0] + NZ // 2) % NZ
    apart = (centre_x - empty_x) ** 2 + (centre_y - empty_y) ** 2 + (centre_z - empty_z) ** 2
    trials = jnp.arange(3 * RADIUS // 2, dtype=jnp.int32)
    largest = jnp.sum((trials[None, :] * trials[None, :] < apart[:, None]).astype(jnp.int32), axis=1) - 1
    first_radius = jnp.minimum(radius_all[0], largest[0])
    grid_x = jnp.arange(NX, dtype=jnp.int32)[:, None, None]
    grid_y = jnp.arange(NY, dtype=jnp.int32)[None, :, None]
    grid_z = jnp.arange(NZ, dtype=jnp.int32)[None, None, :]
    inside = jnp.zeros((NX, NY, NZ), jnp.bool_)
    for which in range(count):
        if which == 0:
            extent = first_radius
        else:
            extent = radius_all[which]
        spread = (grid_x - centre_x[which]) ** 2 + (grid_y - centre_y[which]) ** 2 + (grid_z - centre_z[which]) ** 2
        member = spread <= extent * extent
        if which > 0:
            member = member & (extent * extent < apart[which])
        inside = inside | member
    return inside.astype(jnp.int32)


def level_of(rng, shape, cuts, smallest, high):
    level, own = 1.0, jax.random.fold_in(rng, 6)
    for position, shards_of in cuts:
        steps = jnp.exp(jax.random.uniform(jax.random.fold_in(own, position), (shards_of,), jnp.float32, smallest / len(cuts), high / len(cuts)))
        level = level * jnp.repeat(steps, shape[position] // shards_of).reshape([-1 if axis == position else 1 for axis in range(len(shape))])
    return level


def bell_draw(rng, shape, scale, most, cuts=(), kind=jnp.bfloat16):
    drawn = scale * jax.random.normal(rng, shape, jnp.float32)
    if cuts:
        drawn = drawn * level_of(rng, shape, cuts, -0.22, 0.18)
    return jnp.clip(drawn, -most, most).astype(kind)


def setup_inputs(seed: int = 0) -> dict:
    key_of = jax.random.split(jax.random.key(seed), 4)
    return {
        "features": bell_draw(key_of[0], (CH, NX, NY, NZ), 1.0, 6.0, ((1, 8), (2, 4), (3, 8))),
        "conv_weight": bell_draw(key_of[1], (27, CH), (27 * CH) ** -0.5, 0.21875),
        "mask": draw_mask(jax.random.fold_in(key_of[3], 71), 0),
    }


def window_min(padded, axis, length, radius):
    center = lax.slice_in_dim(padded, radius, radius + length, axis=axis)

    def step(shift, acc):
        shift = jnp.asarray(shift).astype(jnp.int32)
        lower = lax.dynamic_slice_in_dim(padded, (radius - shift).astype(jnp.int32), length, axis)
        upper = lax.dynamic_slice_in_dim(padded, (radius + shift).astype(jnp.int32), length, axis)
        square = (shift * shift).astype(jnp.float32)
        return jnp.minimum(acc, jnp.minimum(lower, upper) + square)

    return lax.fori_loop(1, radius + 1, step, center)


def line_pass(values, axis, radius, ceiling):
    widths = [(0, 0), (0, 0), (0, 0)]
    widths[axis] = (radius, radius)
    padded = jnp.pad(values, widths, constant_values=ceiling)
    return window_min(padded, axis, values.shape[axis], radius)


def reference(features, conv_weight, mask):
    kernel = jnp.transpose(conv_weight).reshape(1, CH, 3, 3, 3)
    score = lax.conv_general_dilated(features[None], kernel, (1, 1, 1), "SAME", dimension_numbers=("NCDHW", "OIDHW", "NCDHW"), preferred_element_type=jnp.float32)[0, 0]
    ceiling = float(RADIUS * RADIUS)
    cost = jnp.where(mask == 1, jnp.float32(ceiling), ceiling * jax.nn.sigmoid(score))
    along_x = line_pass(cost, 0, RADIUS, ceiling)
    along_y = line_pass(along_x, 1, RADIUS, ceiling)
    distance = line_pass(along_y, 2, RADIUS, ceiling)
    return score, distance / RADIUS
```

```python
import functools

import jax
import jax.numpy as jnp
from jax import lax
from jax.experimental import pallas as pl
from jax.experimental.pallas import tpu as pltpu
from jax.sharding import PartitionSpec as P

MESH = pl.DeviceIdType.MESH
RADIUS = 128
CEILING = float(RADIUS * RADIUS)
FAR = 1.0e9
F32 = jnp.float32
BX, BY, BZ = 4, 64, 128
NI, NJ, NK = 8, 4, 8
PLANES = BX + 2
STEPS = RADIUS - 1


def iota(shape, axis):
    return lax.broadcasted_iota(jnp.int32, shape, axis)


def banded_weights(w_ref, wb_ref):
    rows, cols = 9 * 32, 32 * 16
    weights = w_ref[...]
    row = iota((rows, 27), 0)
    tap = iota((rows, 27), 1)
    group = row // 32
    spread = (iota((32, cols), 1) // 16 == iota((32, cols), 0)).astype(jnp.bfloat16)
    gap = iota((rows, cols), 1) % 16 - (iota((rows, cols), 0) % 32 - 8)
    total = jnp.zeros((rows, cols), F32)
    for b in range(3):
        pick = (tap == (group // 3) * 9 + 3 * b + group % 3).astype(jnp.bfloat16)
        own = jnp.dot(pick, weights, preferred_element_type=F32).astype(jnp.bfloat16)
        wide = jnp.dot(own, spread, preferred_element_type=F32)
        total = jnp.where(gap == b - 1, wide, total)
    wb_ref[...] = total.astype(jnp.bfloat16)


def kernel(
    f_ref, w_ref, m_ref, score_ref, depth_ref,
    wb, s3, s, pack, r0, r1, mr, sc, scb, xin, xo, yb, yp, yo, zb, tz,
    r0_send, r0_recv, m_send, m_recv, r1_send, r1_recv, sc_send, sc_recv,
    r2_send, r2_recv, r3_send, r3_recv,
):
    i, j, k = lax.axis_index("gx"), lax.axis_index("gy"), lax.axis_index("gz")

    barrier = pltpu.get_barrier_semaphore()

    def greet(di, dj, dk):
        pl.semaphore_signal(
            barrier, inc=1, device_id=((i + di) % NI, (j + dj) % NJ, (k + dk) % NK), device_id_type=MESH
        )

    greeted = 0
    for di in range(NI):
        for dj in range(NJ):
            if di or dj:
                greet(di, dj, 0)
                greeted += 1
    for dk in (1, NK - 1):
        for dj in range(NJ):
            greet(0, dj, dk)
            greeted += 1

    banded_weights(w_ref, wb)
    s3[...] = jnp.zeros_like(s3)

    def conv_block(q, carry):
        start = pl.multiple_of(q * 16, 16)
        for xs in range(BX):
            block = f_ref[:, xs, pl.ds(start, 16), :].reshape(32 * 16, BZ)
            part = jnp.dot(wb[...], block, preferred_element_type=F32)
            for a in range(3):
                for c in range(3):
                    at = (3 * a + c) * 32
                    s3[c, xs - a + 2, pl.ds(start, 32), :] += part[at : at + 32]
        return carry

    lax.fori_loop(0, BY // 16, conv_block, 0)

    lane = iota((8, BZ), 1)
    sub = iota((8, BZ), 0)
    edge = (lane == 0) | (lane == BZ - 1)
    pack[...] = jnp.zeros_like(pack)

    def shift_plane(p, tile):
        for t in range(10):
            rows = pl.ds(8 * t, 8)
            right = pltpu.roll(s3[0, p, rows, :], 1, 1)
            left = pltpu.roll(s3[2, p, rows, :], BZ - 1, 1)
            mine = s3[1, p, rows, :] + jnp.where(lane == 0, 0.0, right) + jnp.where(lane == BZ - 1, 0.0, left)
            s[p, rows, :] = mine
            rim = jnp.where(lane == 0, right, left)
            if t == 0:
                pack[1, pl.ds(p, 1), :] = mine[7:8]
                pack[2, pl.ds(p, 1), :] = rim[7:8]
            elif t == 9:
                pack[3, pl.ds(p, 1), :] = mine[0:1]
                pack[4, pl.ds(p, 1), :] = rim[0:1]
            else:
                v = 2 * (p * 8 + t - 1)
                moved = pltpu.roll(rim, v, 1)
                tile = jnp.where((lane == v) | (lane == (v + BZ - 1) % BZ), moved, tile)
        return tile

    pack[0] = lax.fori_loop(0, PLANES, shift_plane, jnp.zeros((8, BZ), F32))

    pl.semaphore_wait(barrier, greeted)

    def mask_rows(step, carry):
        to = (i + step) % NI
        pltpu.make_async_remote_copy(
            m_ref.at[:, pl.ds(pl.multiple_of(to * 8, 8), 8), :], mr.at[i], m_send, m_recv,
            device_id=(to, j, k), device_id_type=MESH,
        ).start()
        return carry

    slot = 0
    halo = []
    for dj, dk, source in (
        (0, 1, 0), (0, -1, 0), (-1, 0, 1), (-1, 1, 2), (-1, -1, 2), (1, 0, 3), (1, 1, 4), (1, -1, 4)
    ):
        copy = pltpu.make_async_remote_copy(
            pack.at[source], r0.at[slot], r0_send.at[slot], r0_recv.at[slot],
            device_id=(i, (j + dj) % NJ, (k + dk) % NK), device_id_type=MESH,
        )
        copy.start()
        halo.append(copy)
        slot += 1
    lax.fori_loop(1, NI, mask_rows, 0)
    pltpu.make_async_copy(m_ref.at[:, pl.ds(pl.multiple_of(i * 8, 8), 8), :], mr.at[i], m_recv).start()
    for copy in halo:
        copy.wait()

    first_z, last_z, first_y, last_y = k == 0, k == NK - 1, j == 0, j == NJ - 1
    zero = jnp.zeros((8, BZ), F32)

    def unless(absent, value):
        return jnp.where(absent, zero, value)

    lower, upper = unless(first_z, r0[0]), unless(last_z, r0[1])
    both = jnp.where(lane % 2 == 0, lower, upper)
    below = r0[2] + jnp.where(lane == 0, unless(first_z, r0[3]), 0.0)
    below = unless(last_y, below + jnp.where(lane == BZ - 1, unless(last_z, r0[4]), 0.0))
    above = r0[5] + jnp.where(lane == 0, unless(first_z, r0[6]), 0.0)
    above = unless(first_y, above + jnp.where(lane == BZ - 1, unless(last_z, r0[7]), 0.0))
    pack[1] = below
    pack[2] = above

    def add_halo(p, carry):
        for t in range(1, 9):
            rows = pl.ds(8 * t, 8)
            v = 2 * (p * 8 + t - 1)
            moved = pltpu.roll(both, (2 * BZ - v) % BZ, 1)
            value = s[p, rows, :] + jnp.where(edge, moved, 0.0)
            if t == 1:
                value += jnp.where(sub == 0, pack[2, pl.ds(p, 1), :], 0.0)
            if t == 8:
                value += jnp.where(sub == 7, pack[1, pl.ds(p, 1), :], 0.0)
            s[p, rows, :] = value
        return carry

    lax.fori_loop(0, PLANES, add_halo, 0)

    def part_rows(to):
        return s.at[:, pl.ds(pl.multiple_of(8 + to * 8, 8), 8), :]

    def send_parts(step, carry):
        to = (i + step) % NI
        pltpu.make_async_remote_copy(
            part_rows(to), r1.at[i], r1_send, r1_recv, device_id=(to, j, k), device_id_type=MESH
        ).start()
        return carry

    lax.fori_loop(1, NI, send_parts, 0)
    pltpu.make_async_copy(part_rows(i), r1.at[i], r1_recv).start()
    pltpu.make_async_copy(r1, r1, r1_recv).wait()
    pltpu.make_async_copy(mr, mr, m_recv).wait()

    for b in range(NI):
        for a in range(BX):
            value = r1[b, a + 1]
            if a == 0 and b > 0:
                value += r1[b - 1, BX + 1]
            if a == BX - 1 and b < NI - 1:
                value += r1[b + 1, 0]
            x = BX * b + a
            sc[x] = value
            cost = CEILING / (1.0 + jnp.exp(-value))
            xin[32 + x] = jnp.where(mr[b, a] == 1, CEILING, cost)

    def send_scores(step, carry):
        to = (i + step) % NI
        pltpu.make_async_remote_copy(
            sc.at[pl.ds(to * BX, BX)], scb.at[i], sc_send, sc_recv, device_id=(to, j, k), device_id_type=MESH
        ).start()
        return carry

    lax.fori_loop(1, NI, send_scores, 0)
    pltpu.make_async_copy(sc.at[pl.ds(i * BX, BX)], scb.at[i], sc_recv).start()

    far = jnp.full((32, 8, BZ), FAR, F32)
    xin[0:32] = far
    xin[64:96] = far

    def step_x(n, acc):
        square = (n * n).astype(F32)
        return jnp.minimum(acc, jnp.minimum(xin[pl.ds(32 - n, 32)], xin[pl.ds(32 + n, 32)]) + square)

    xo[...] = lax.fori_loop(1, 32, step_x, xin[32:64])

    def send_x(step, carry):
        peer = (i * NJ + j + step) % (NI * NJ)
        ti, tj = peer // NJ, peer % NJ
        pltpu.make_async_remote_copy(
            xo.at[peer], yb.at[j * NI + i], r2_send, r2_recv, device_id=(ti, tj, k), device_id_type=MESH
        ).start()
        return carry

    lax.fori_loop(1, NI * NJ, send_x, 0)
    pltpu.make_async_copy(xo.at[i * NJ + j], yb.at[j * NI + i], r2_recv).start()

    edge_rows = jnp.full((128, BZ), FAR, F32)
    yp[0:128] = edge_rows
    yp[384:512] = edge_rows
    pltpu.make_async_copy(yb, yb, r2_recv).wait()
    yp[128:384] = yb[...].reshape(256, BZ)

    def step_y(n, acc):
        square = (n * n).astype(F32)
        low = yp[pl.ds(128 - n, 256), :]
        high = yp[pl.ds(128 + n, 256), :]
        return jnp.minimum(acc, jnp.minimum(low, high) + square)

    yo[...] = lax.fori_loop(1, STEPS + 1, step_y, yp[128:384])

    def y_rows(to):
        return yo.at[pl.ds(pl.multiple_of(to * BY, BY), BY), :]

    for dj in range(NJ):
        for dk in (1, -1, 0):
            to = (j + dj) % NJ
            if dj == 0 and dk == 0:
                pltpu.make_async_copy(y_rows(to), zb.at[NJ + j], r3_recv).start()
            else:
                pltpu.make_async_remote_copy(
                    y_rows(to), zb.at[NJ * (1 - dk) + j], r3_send, r3_recv,
                    device_id=(i, to, (k + dk) % NK), device_id_type=MESH,
                ).start()
    pltpu.make_async_copy(zb, zb, r3_recv).wait()

    for d in range(3):
        for h in range(2):
            turned = zb[NJ * d + 2 * h : NJ * d + 2 * h + 2].reshape(128, BZ).T
            if d == 0:
                turned = jnp.where(first_z, FAR, turned)
            if d == 2:
                turned = jnp.where(last_z, FAR, turned)
            tz[h, 128 * d : 128 * d + 128, :] = turned

    def step_z(n, acc):
        square = (n * n).astype(F32)
        low = tz[:, pl.ds(128 - n, 128), :]
        high = tz[:, pl.ds(128 + n, 128), :]
        return jnp.minimum(acc, jnp.minimum(low, high) + square)

    least = lax.fori_loop(1, STEPS + 1, step_z, tz[:, 128:256, :])
    for h in range(2):
        depth_ref[2 * h : 2 * h + 2] = (least[h] * (1.0 / RADIUS)).T.reshape(2, BY, BZ)

    pltpu.make_async_copy(scb, scb, sc_recv).wait()
    for b in range(NI):
        score_ref[:, 8 * b : 8 * b + 8, :] = scb[b]

    seven = pl.ds(0, NI - 1)
    pltpu.make_async_copy(mr.at[seven], mr.at[seven], m_send).wait()
    pltpu.make_async_copy(r1.at[seven], r1.at[seven], r1_send).wait()
    pltpu.make_async_copy(scb.at[seven], scb.at[seven], sc_send).wait()
    most = pl.ds(0, NI * NJ - 1)
    pltpu.make_async_copy(yb.at[most], yb.at[most], r2_send).wait()
    most = pl.ds(0, 3 * NJ - 1)
    pltpu.make_async_copy(zb.at[most], zb.at[most], r3_send).wait()


def shards(features, conv_weight, mask):
    vmem = pl.BlockSpec(memory_space=pltpu.VMEM)
    tile = (8, BZ)
    dma = pltpu.SemaphoreType.DMA
    out = jax.ShapeDtypeStruct((BX, BY, BZ), F32)
    return pl.pallas_call(
        kernel,
        out_shape=(out, out),
        in_specs=[vmem] * 3,
        out_specs=(vmem, vmem),
        scratch_shapes=[
            pltpu.VMEM((288, 512), jnp.bfloat16),
            pltpu.VMEM((3, PLANES, BY + 16, BZ), F32),
            pltpu.VMEM((PLANES, BY + 16, BZ), F32),
            pltpu.VMEM((5, *tile), F32),
            pltpu.VMEM((8, *tile), F32),
            pltpu.VMEM((NI, PLANES, *tile), F32),
            pltpu.VMEM((NI, BX, *tile), jnp.int32),
            pltpu.VMEM((32, *tile), F32),
            pltpu.VMEM((NI, BX, *tile), F32),
            pltpu.VMEM((96, *tile), F32),
            pltpu.VMEM((32, *tile), F32),
            pltpu.VMEM((32, *tile), F32),
            pltpu.VMEM((512, BZ), F32),
            pltpu.VMEM((256, BZ), F32),
            pltpu.VMEM((3 * NJ, BY, BZ), F32),
            pltpu.VMEM((2, 384, BZ), F32),
            dma((8,)), dma((8,)),
        ] + [dma] * 10,
        compiler_params=pltpu.CompilerParams(
            collective_id=0, has_side_effects=True, vmem_limit_bytes=40 * 1024 * 1024
        ),
    )(features, conv_weight, mask)


def solution(mesh):
    in_specs = (P(None, "gx", "gy", "gz"), P(), P("gx", "gy", "gz"))
    out_specs = (P("gx", "gy", "gz"), P("gx", "gy", "gz"))
    return jax.shard_map(shards, mesh=mesh, in_specs=in_specs, out_specs=out_specs, check_vma=False)
```

```python
import functools

import jax
import jax.numpy as jnp
from jax import lax
from jax.experimental import pallas as pl
from jax.experimental.pallas import tpu as pltpu
from jax.sharding import PartitionSpec as P

MESH = pl.DeviceIdType.MESH
RADIUS = 128
CEILING = float(RADIUS * RADIUS)
FAR = 1.0e9
F32 = jnp.float32
BX, BY, BZ = 4, 64, 128
NI, NJ, NK = 8, 4, 8
PLANES = BX + 2
STEPS = RADIUS - 1


def iota(shape, axis):
    return lax.broadcasted_iota(jnp.int32, shape, axis)


def banded_weights(w_ref, wb_ref):
    rows, cols = 9 * 32, 32 * 16
    weights = w_ref[...]
    row = iota((rows, 27), 0)
    tap = iota((rows, 27), 1)
    group = row // 32
    spread = (iota((32, cols), 1) // 16 == iota((32, cols), 0)).astype(jnp.bfloat16)
    gap = iota((rows, cols), 1) % 16 - (iota((rows, cols), 0) % 32 - 8)
    total = jnp.zeros((rows, cols), F32)
    for b in range(3):
        pick = (tap == (group // 3) * 9 + 3 * b + group % 3).astype(jnp.bfloat16)
        own = jnp.dot(pick, weights, preferred_element_type=F32).astype(jnp.bfloat16)
        wide = jnp.dot(own, spread, preferred_element_type=F32)
        total = jnp.where(gap == b - 1, wide, total)
    wb_ref[...] = total.astype(jnp.bfloat16)


def kernel(
    f_hbm, w_hbm, m_hbm, score_ref, depth_ref,
    f_ref, w_ref, m_ref, wb, s3, s, pack, r1, rims, rows_in, mr, sc, scb, xin, xo, yb, yp, yo, zb, tz,
    in_sems, m_send, m_recv, r1_send, r1_recv, t_send, t_recv, row_send, row_recv, sc_send, sc_recv,
    r2_send, r2_recv, r3_send, r3_recv,
):
    i, j, k = lax.axis_index("gx"), lax.axis_index("gy"), lax.axis_index("gz")
    loads = [
        pltpu.make_async_copy(source, target, in_sems.at[n])
        for n, (source, target) in enumerate(((w_hbm, w_ref), (f_hbm, f_ref), (m_hbm, m_ref)))
    ]
    for load in loads:
        load.start()

    barrier = pltpu.get_barrier_semaphore()

    def greet(di, dj, dk):
        pl.semaphore_signal(
            barrier, inc=1, device_id=((i + di) % NI, (j + dj) % NJ, (k + dk) % NK), device_id_type=MESH
        )

    def greet_plane(step, carry):
        greet(step // NJ, step % NJ, 0)
        return carry

    def greet_sides(step, carry):
        greet(step % NI, 0, 1)
        greet(step % NI, 0, NK - 1)
        return carry

    def greet_lines(step, carry):
        greet(0, step, 1)
        greet(0, step, NK - 1)
        return carry

    lax.fori_loop(1, NI * NJ, greet_plane, 0)
    lax.fori_loop(0, NI, greet_sides, 0)
    lax.fori_loop(1, NJ, greet_lines, 0)
    at_end = (i == 0) | (i == NI - 1)

    @pl.when(at_end)
    def _():
        dj = jnp.where(i == 0, NJ - 1, 1)

        def greet_corners(step, carry):
            greet(step, dj, 1)
            greet(step, dj, NK - 1)
            return carry

        lax.fori_loop(0, NI, greet_corners, 0)

    greeted = NI * NJ - 1 + 2 * NI + 2 * (NJ - 1) + 4

    loads[0].wait()
    banded_weights(w_ref, wb)
    s3[...] = jnp.zeros_like(s3)
    loads[1].wait()

    def conv_block(q, carry):
        start = pl.multiple_of(q * 16, 16)
        for xs in range(BX):
            block = f_ref[:, xs, pl.ds(start, 16), :].reshape(32 * 16, BZ)
            part = jnp.dot(wb[...], block, preferred_element_type=F32)
            for a in range(3):
                for c in range(3):
                    at = (3 * a + c) * 32
                    s3[c, xs - a + 2, pl.ds(start, 32), :] += part[at : at + 32]
        return carry

    lax.fori_loop(0, BY // 16, conv_block, 0)

    lane = iota((8, BZ), 1)
    sub = iota((8, BZ), 0)
    edge = (lane == 0) | (lane == BZ - 1)
    zero = jnp.zeros((8, BZ), F32)
    pack[...] = jnp.zeros_like(pack)

    def shift_plane(p, tile):
        for t in range(10):
            rows = pl.ds(8 * t, 8)
            right = pltpu.roll(s3[0, p, rows, :], 1, 1)
            left = pltpu.roll(s3[2, p, rows, :], BZ - 1, 1)
            mine = s3[1, p, rows, :] + jnp.where(lane == 0, 0.0, right) + jnp.where(lane == BZ - 1, 0.0, left)
            s[p, rows, :] = mine
            rim = jnp.where(lane == 0, right, left)
            if t == 0:
                pack[1, pl.ds(p, 1), :] = mine[7:8]
                pack[2, pl.ds(p, 1), :] = rim[7:8]
            elif t == 9:
                pack[3, pl.ds(p, 1), :] = mine[0:1]
                pack[4, pl.ds(p, 1), :] = rim[0:1]
            else:
                v = 2 * (p * 8 + t - 1)
                moved = pltpu.roll(rim, v, 1)
                tile = jnp.where((lane == v) | (lane == (v + BZ - 1) % BZ), moved, tile)
        return tile

    pack[0] = lax.fori_loop(0, PLANES, shift_plane, zero)
    far = jnp.full((128, BZ), FAR, F32)
    yp[0:128] = far
    yp[384:512] = far

    @pl.when(jnp.logical_not(at_end))
    def _():
        rows_in[...] = jnp.zeros_like(rows_in)

    loads[2].wait()
    pl.semaphore_wait(barrier, greeted)

    def part_rows(to):
        return s.at[:, pl.ds(pl.multiple_of(8 + to * 8, 8), 8), :]

    def mask_rows(to):
        return m_ref.at[:, pl.ds(pl.multiple_of(to * 8, 8), 8), :]

    def remote(source, target, send, recv, device):
        pltpu.make_async_remote_copy(
            source, target, send, recv, device_id=device, device_id_type=MESH
        ).start()

    def send_parts(step, carry):
        to = (i + step) % NI
        remote(part_rows(to), r1.at[i], r1_send, r1_recv, (to, j, k))
        remote(pack.at[0], rims.at[i], t_send, t_recv, (to, j, (k + 1) % NK))
        remote(pack.at[0], rims.at[NI + i], t_send, t_recv, (to, j, (k + NK - 1) % NK))
        remote(mask_rows(to), mr.at[i], m_send, m_recv, (to, j, k))
        return carry

    for ti, dj, near in ((NI - 1, -1, 1), (0, 1, 3)):
        tj = (j + dj) % NJ
        remote(pack.at[near + 1], rows_in.at[NI + i], row_send, row_recv, (ti, tj, (k + 1) % NK))
        remote(pack.at[near + 1], rows_in.at[2 * NI + i], row_send, row_recv, (ti, tj, (k + NK - 1) % NK))
        remote(pack.at[near], rows_in.at[i], row_send, row_recv, (ti, tj, k))
    lax.fori_loop(1, NI, send_parts, 0)
    remote(pack.at[0], rims.at[i], t_send, t_recv, (i, j, (k + 1) % NK))
    remote(pack.at[0], rims.at[NI + i], t_send, t_recv, (i, j, (k + NK - 1) % NK))
    pltpu.make_async_copy(part_rows(i), r1.at[i], r1_recv).start()
    pltpu.make_async_copy(mask_rows(i), mr.at[i], m_recv).start()

    first_z, last_z = k == 0, k == NK - 1
    outside = ((i == 0) & (j == 0)) | ((i == NI - 1) & (j == NJ - 1))

    def drain(ref, semaphore):
        pltpu.make_async_copy(ref, ref, semaphore).wait()

    @pl.when(at_end)
    def _():
        drain(rows_in, row_recv)

    drain(r1, r1_recv)
    drain(rims, t_recv)
    drain(mr, m_recv)

    end_row = sub == jnp.where(i == 0, 0, 7)
    parts = []
    for b in range(NI):
        both = jnp.where(
            lane % 2 == 0, jnp.where(first_z, zero, rims[b]), jnp.where(last_z, zero, rims[NI + b])
        )
        both = pltpu.roll(both, (2 * BZ - 2 * i) % BZ, 1)
        rows = rows_in[b] + jnp.where((lane == 0) & jnp.logical_not(first_z), rows_in[NI + b], 0.0)
        rows += jnp.where((lane == BZ - 1) & jnp.logical_not(last_z), rows_in[2 * NI + b], 0.0)
        rows = jnp.where(outside, zero, rows)
        planes = []
        for p in range(PLANES):
            moved = both if p == 0 else pltpu.roll(both, BZ - 16 * p, 1)
            planes.append(
                r1[b, p]
                + jnp.where(edge, moved, 0.0)
                + jnp.where(end_row, jnp.broadcast_to(rows[p : p + 1], (8, BZ)), 0.0)
            )
        parts.append(planes)
    for b in range(NI):
        for a in range(BX):
            value = parts[b][a + 1]
            if a == 0 and b > 0:
                value += parts[b - 1][BX + 1]
            if a == BX - 1 and b < NI - 1:
                value += parts[b + 1][0]
            x = BX * b + a
            sc[x] = value
            cost = CEILING / (1.0 + jnp.exp(-value))
            xin[x] = jnp.where(mr[b, a] == 1, CEILING, cost)

    acc = xin[...]
    for n in range(1, 32):
        square = float(n * n)
        if n < 16:
            pair = jnp.minimum(xin[0 : 32 - 2 * n], xin[2 * n : 32]) + square
            least = jnp.concatenate([xin[n : 2 * n] + square, pair, xin[32 - 2 * n : 32 - n] + square], axis=0)
            acc = jnp.minimum(acc, least)
        else:
            low = jnp.minimum(acc[0 : 32 - n], xin[n:32] + square)
            high = jnp.minimum(acc[n:32], xin[0 : 32 - n] + square)
            middle = [acc[32 - n : n]] if n > 16 else []
            acc = jnp.concatenate([low, *middle, high], axis=0)
    xo[...] = acc

    def send_x(step, carry):
        peer = (i * NJ + j + step) % (NI * NJ)
        remote(xo.at[peer], yb.at[j * NI + i], r2_send, r2_recv, (peer // NJ, peer % NJ, k))
        return carry

    lax.fori_loop(1, NI * NJ, send_x, 0)
    pltpu.make_async_copy(xo.at[i * NJ + j], yb.at[j * NI + i], r2_recv).start()

    def send_scores(step, carry):
        to = (i + step) % NI
        remote(sc.at[pl.ds(to * BX, BX)], scb.at[i], sc_send, sc_recv, (to, j, k))
        return carry

    lax.fori_loop(1, NI, send_scores, 0)
    pltpu.make_async_copy(sc.at[pl.ds(i * BX, BX)], scb.at[i], sc_recv).start()

    drain(yb, r2_recv)
    yp[128:384] = yb[...].reshape(256, BZ)

    for turn, to in enumerate(((j + 2) % NJ, NJ - 1 - j, j + 1 - 2 * (j % 2), j)):
        base = pl.multiple_of(128 + to * BY, BY)

        def step_y(n, acc):
            square = (n * n).astype(F32)
            low = yp[pl.ds(base - n, BY), :]
            high = yp[pl.ds(base + n, BY), :]
            return jnp.minimum(acc, jnp.minimum(low, high) + square)

        yo[turn] = lax.fori_loop(1, STEPS + 2, step_y, yp[pl.ds(base, BY), :], unroll=8)
        for dk in (1, -1, 0):
            if turn == 3 and dk == 0:
                pltpu.make_async_copy(yo.at[turn], zb.at[NJ + j], r3_recv).start()
            else:
                remote(
                    yo.at[turn], zb.at[NJ * (1 - dk) + j], r3_send, r3_recv, (i, to, (k + dk) % NK)
                )

    drain(scb, sc_recv)
    for b in range(NI):
        score_ref[:, 8 * b : 8 * b + 8, :] = scb[b]
    drain(zb, r3_recv)

    for h in range(2):
        for d in range(3):
            turned = zb[NJ * d + 2 * h : NJ * d + 2 * h + 2].reshape(128, BZ).T
            if d == 0:
                turned = jnp.where(first_z, FAR, turned)
            if d == 2:
                turned = jnp.where(last_z, FAR, turned)
            tz[h, 128 * d : 128 * d + 128, :] = turned

        def step_z(n, acc):
            square = (n * n).astype(F32)
            low = tz[h, pl.ds(128 - n, 128), :]
            high = tz[h, pl.ds(128 + n, 128), :]
            return jnp.minimum(acc, jnp.minimum(low, high) + square)

        least = lax.fori_loop(1, STEPS + 2, step_z, tz[h, 128:256, :], unroll=4)
        depth_ref[2 * h : 2 * h + 2] = (least * (1.0 / RADIUS)).T.reshape(2, BY, BZ)

    seven = pl.ds(0, NI - 1)
    drain(mr.at[seven], m_send)
    drain(r1.at[seven], r1_send)
    drain(scb.at[seven], sc_send)
    drain(rims, t_send)
    drain(rows_in.at[pl.ds(0, 6)], row_send)
    drain(yb.at[pl.ds(0, NI * NJ - 1)], r2_send)
    drain(zb.at[pl.ds(0, 3 * NJ - 1)], r3_send)


def shards(features, conv_weight, mask):
    vmem = pl.BlockSpec(memory_space=pltpu.VMEM)
    hbm = pl.BlockSpec(memory_space=pltpu.HBM)
    tile = (8, BZ)
    dma = pltpu.SemaphoreType.DMA
    out = jax.ShapeDtypeStruct((BX, BY, BZ), F32)
    return pl.pallas_call(
        kernel,
        out_shape=(out, out),
        in_specs=[hbm] * 3,
        out_specs=(vmem, vmem),
        scratch_shapes=[
            pltpu.VMEM((32, BX, BY, BZ), jnp.bfloat16),
            pltpu.VMEM((27, 32), jnp.bfloat16),
            pltpu.VMEM((BX, BY, BZ), jnp.int32),
            pltpu.VMEM((288, 512), jnp.bfloat16),
            pltpu.VMEM((3, PLANES, BY + 16, BZ), F32),
            pltpu.VMEM((PLANES, BY + 16, BZ), F32),
            pltpu.VMEM((5, *tile), F32),
            pltpu.VMEM((NI, PLANES, *tile), F32),
            pltpu.VMEM((2 * NI, *tile), F32),
            pltpu.VMEM((3 * NI, *tile), F32),
            pltpu.VMEM((NI, BX, *tile), jnp.int32),
            pltpu.VMEM((32, *tile), F32),
            pltpu.VMEM((NI, BX, *tile), F32),
            pltpu.VMEM((32, *tile), F32),
            pltpu.VMEM((32, *tile), F32),
            pltpu.VMEM((32, *tile), F32),
            pltpu.VMEM((512, BZ), F32),
            pltpu.VMEM((NJ, BY, BZ), F32),
            pltpu.VMEM((3 * NJ, BY, BZ), F32),
            pltpu.VMEM((2, 384, BZ), F32),
            dma((3,)),
        ] + [dma] * 14,
        compiler_params=pltpu.CompilerParams(
            collective_id=0, has_side_effects=True, vmem_limit_bytes=40 * 1024 * 1024
        ),
    )(features, conv_weight, mask)


def solution(mesh):
    in_specs = (P(None, "gx", "gy", "gz"), P(), P("gx", "gy", "gz"))
    out_specs = (P("gx", "gy", "gz"), P("gx", "gy", "gz"))
    return jax.shard_map(shards, mesh=mesh, in_specs=in_specs, out_specs=out_specs, check_vma=False)
```

```python
import functools

import jax
import jax.numpy as jnp
from jax import lax
from jax.experimental import pallas as pl
from jax.experimental.pallas import tpu as pltpu
from jax.sharding import PartitionSpec as P

MESH = pl.DeviceIdType.MESH
RADIUS = 128
CEILING = float(RADIUS * RADIUS)
FAR = 1.0e9
F32 = jnp.float32
BX, BY, BZ = 4, 64, 128
NI, NJ, NK = 8, 4, 8
PLANES = BX + 2
STEPS = RADIUS - 1


def iota(shape, axis):
    return lax.broadcasted_iota(jnp.int32, shape, axis)


def banded_weights(w_ref, wb_ref):
    rows, cols = 9 * 32, 32 * 16
    weights = w_ref[...]
    row = iota((rows, 27), 0)
    tap = iota((rows, 27), 1)
    group = row // 32
    spread = (iota((32, cols), 1) // 16 == iota((32, cols), 0)).astype(jnp.bfloat16)
    gap = iota((rows, cols), 1) % 16 - (iota((rows, cols), 0) % 32 - 8)
    total = jnp.zeros((rows, cols), F32)
    for b in range(3):
        pick = (tap == (group // 3) * 9 + 3 * b + group % 3).astype(jnp.bfloat16)
        own = jnp.dot(pick, weights, preferred_element_type=F32).astype(jnp.bfloat16)
        wide = jnp.dot(own, spread, preferred_element_type=F32)
        total = jnp.where(gap == b - 1, wide, total)
    wb_ref[...] = total.astype(jnp.bfloat16)


def kernel(
    f_hbm, w_hbm, m_hbm, score_ref, depth_ref,
    f_ref, w_ref, m_ref, wb, s3, s, pack, r1, rims, rims_y, rows_in, mr, sc, scb, xin, xo, yb, yp, yo, zb, tz,
    in_sems, m_send, m_recv, r1_send, r1_recv, row_send, row_recv, sc_send, sc_recv,
    r2_send, r2_recv, t_send, t_recv, ry_send, ry_recv, r3_send, r3_recv,
):
    i, j, k = lax.axis_index("gx"), lax.axis_index("gy"), lax.axis_index("gz")
    loads = [
        pltpu.make_async_copy(source, target, in_sems.at[n])
        for n, (source, target) in enumerate(((w_hbm, w_ref), (f_hbm, f_ref), (m_hbm, m_ref)))
    ]
    for load in loads:
        load.start()

    def around(position, size):
        return [position] + [
            jnp.where(position >= size - d, position - (size - d), position + d) for d in range(1, size)
        ]

    xs_of, ys_of = around(i, NI), around(j, NJ)
    first_z, last_z = k == 0, k == NK - 1
    sides = ((1, k + 1, jnp.logical_not(last_z)), (0, k - 1, jnp.logical_not(first_z)))
    side_count = 2 - first_z.astype(jnp.int32) - last_z.astype(jnp.int32)

    barrier = pltpu.get_barrier_semaphore()

    def greet(*device):
        pl.semaphore_signal(barrier, inc=1, device_id=device, device_id_type=MESH)

    for _, tk, there in sides:
        @pl.when(there)
        def _():
            for ti in xs_of:
                greet(ti, j, tk)
            for tj in ys_of[1:]:
                greet(i, tj, tk)

    for ti in xs_of:
        for tj in ys_of:
            if ti is not i or tj is not j:
                greet(ti, tj, k)
    at_end = (i == 0) | (i == NI - 1)

    end_j = jnp.where(i == 0, ys_of[NJ - 1], ys_of[1])
    for _, tk, there in sides:
        @pl.when(there & at_end)
        def _():
            for ti in range(NI):
                greet(ti, end_j, tk)

    greeted = NI * NJ - 1 + side_count * (NI + NJ - 1 + 2)

    loads[0].wait()
    banded_weights(w_ref, wb)
    s3[...] = jnp.zeros_like(s3)
    loads[1].wait()

    def conv_block(q, carry):
        start = pl.multiple_of(q * 16, 16)
        for xs in range(BX):
            block = f_ref[:, xs, pl.ds(start, 16), :].reshape(32 * 16, BZ)
            part = jnp.dot(wb[...], block, preferred_element_type=F32)
            for a in range(3):
                for c in range(3):
                    at = (3 * a + c) * 32
                    s3[c, xs - a + 2, pl.ds(start, 32), :] += part[at : at + 32]
        return carry

    lax.fori_loop(0, BY // 16, conv_block, 0)

    lane = iota((8, BZ), 1)
    sub = iota((8, BZ), 0)
    edge = (lane == 0) | (lane == BZ - 1)
    zero = jnp.zeros((8, BZ), F32)
    pack[...] = jnp.zeros_like(pack)

    def shift_plane(p, tile):
        for t in range(10):
            rows = pl.ds(8 * t, 8)
            right = pltpu.roll(s3[0, p, rows, :], 1, 1)
            left = pltpu.roll(s3[2, p, rows, :], BZ - 1, 1)
            mine = s3[1, p, rows, :] + jnp.where(lane == 0, 0.0, right) + jnp.where(lane == BZ - 1, 0.0, left)
            s[p, rows, :] = mine
            rim = jnp.where(lane == 0, right, left)
            if t == 0:
                pack[1, pl.ds(p, 1), :] = mine[7:8]
                pack[2, pl.ds(p, 1), :] = rim[7:8]
            elif t == 9:
                pack[3, pl.ds(p, 1), :] = mine[0:1]
                pack[4, pl.ds(p, 1), :] = rim[0:1]
            else:
                v = 2 * (p * 8 + t - 1)
                moved = pltpu.roll(rim, v, 1)
                tile = jnp.where((lane == v) | (lane == (v + BZ - 1) % BZ), moved, tile)
        return tile

    pack[0] = lax.fori_loop(0, PLANES, shift_plane, zero)
    far = jnp.full((128, BZ), FAR, F32)
    yp[0:128] = far
    yp[384:512] = far

    @pl.when(jnp.logical_not(at_end))
    def _():
        rows_in[...] = jnp.zeros_like(rows_in)
        rims_y[...] = jnp.zeros_like(rims_y)

    loads[2].wait()
    pl.semaphore_wait(barrier, greeted)

    def part_rows(to):
        return s.at[:, pl.ds(pl.multiple_of(8 + to * 8, 8), 8), :]

    def mask_rows(to):
        return m_ref.at[:, pl.ds(pl.multiple_of(to * 8, 8), 8), :]

    def remote(source, target, send, recv, device):
        pltpu.make_async_remote_copy(
            source, target, send, recv, device_id=device, device_id_type=MESH
        ).start()

    ends = ((NI - 1, ys_of[NJ - 1], 1), (0, ys_of[1], 3))
    for after, tk, there in sides:
        @pl.when(there)
        def _():
            for ti, tj, near in ends:
                remote(
                    pack.at[near + 1], rims_y.at[1 - after, i], ry_send.at[after], ry_recv.at[1 - after],
                    (ti, tj, tk),
                )
            for ti in xs_of:
                remote(pack.at[0], rims.at[1 - after, i], t_send.at[after], t_recv.at[1 - after], (ti, j, tk))

    for ti, tj, near in ends:
        remote(pack.at[near], rows_in.at[i], row_send, row_recv, (ti, tj, k))
    for ti in xs_of[1:]:
        remote(mask_rows(ti), mr.at[i], m_send, m_recv, (ti, j, k))
        remote(part_rows(ti), r1.at[i], r1_send, r1_recv, (ti, j, k))
    pltpu.make_async_copy(part_rows(i), r1.at[i], r1_recv).start()
    pltpu.make_async_copy(mask_rows(i), mr.at[i], m_recv).start()

    outside = ((i == 0) & (j == 0)) | ((i == NI - 1) & (j == NJ - 1))

    def drain(ref, semaphore):
        pltpu.make_async_copy(ref, ref, semaphore).wait()

    @pl.when(at_end)
    def _():
        drain(rows_in, row_recv)

    for after, tk, there in sides:
        @pl.when(there & at_end)
        def _():
            drain(rims_y.at[after], ry_recv.at[after])

        @pl.when(there)
        def _():
            drain(rims.at[after], t_recv.at[after])

    drain(r1, r1_recv)
    drain(mr, m_recv)

    end_row = sub == jnp.where(i == 0, 0, 7)
    parts = []
    for b in range(NI):
        both = jnp.where(
            lane % 2 == 0, jnp.where(first_z, zero, rims[0, b]), jnp.where(last_z, zero, rims[1, b])
        )
        both = pltpu.roll(both, (2 * BZ - 2 * i) % BZ, 1)
        rows = rows_in[b] + jnp.where((lane == 0) & jnp.logical_not(first_z), rims_y[0, b], 0.0)
        rows += jnp.where((lane == BZ - 1) & jnp.logical_not(last_z), rims_y[1, b], 0.0)
        rows = jnp.where(outside, zero, rows)
        planes = []
        for p in range(PLANES):
            moved = both if p == 0 else pltpu.roll(both, BZ - 16 * p, 1)
            planes.append(
                r1[b, p]
                + jnp.where(edge, moved, 0.0)
                + jnp.where(end_row, jnp.broadcast_to(rows[p : p + 1], (8, BZ)), 0.0)
            )
        parts.append(planes)
    for b in range(NI):
        for a in range(BX):
            value = parts[b][a + 1]
            if a == 0 and b > 0:
                value += parts[b - 1][BX + 1]
            if a == BX - 1 and b < NI - 1:
                value += parts[b + 1][0]
            x = BX * b + a
            sc[x] = value
            cost = CEILING / (1.0 + jnp.exp(-value))
            xin[x] = jnp.where(mr[b, a] == 1, CEILING, cost)

    acc = xin[...]
    for n in range(1, 32):
        square = float(n * n)
        if n < 16:
            pair = jnp.minimum(xin[0 : 32 - 2 * n], xin[2 * n : 32]) + square
            least = jnp.concatenate([xin[n : 2 * n] + square, pair, xin[32 - 2 * n : 32 - n] + square], axis=0)
            acc = jnp.minimum(acc, least)
        else:
            low = jnp.minimum(acc[0 : 32 - n], xin[n:32] + square)
            high = jnp.minimum(acc[n:32], xin[0 : 32 - n] + square)
            middle = [acc[32 - n : n]] if n > 16 else []
            acc = jnp.concatenate([low, *middle, high], axis=0)
    xo[...] = acc

    for ti in xs_of:
        for tj in ys_of:
            if ti is not i or tj is not j:
                remote(xo.at[ti * NJ + tj], yb.at[j * NI + i], r2_send, r2_recv, (ti, tj, k))
    pltpu.make_async_copy(xo.at[i * NJ + j], yb.at[j * NI + i], r2_recv).start()

    for ti in xs_of[1:]:
        remote(sc.at[pl.ds(ti * BX, BX)], scb.at[i], sc_send, sc_recv, (ti, j, k))
    pltpu.make_async_copy(sc.at[pl.ds(i * BX, BX)], scb.at[i], sc_recv).start()

    drain(yb, r2_recv)
    yp[128:384] = yb[...].reshape(256, BZ)

    for turn, to in enumerate((ys_of[2], NJ - 1 - j, NJ - 1 - ys_of[2], j)):
        base = pl.multiple_of(128 + to * BY, BY)

        def step_y(n, acc):
            square = (n * n).astype(F32)
            low = yp[pl.ds(base - n, BY), :]
            high = yp[pl.ds(base + n, BY), :]
            return jnp.minimum(acc, jnp.minimum(low, high) + square)

        yo[turn] = lax.fori_loop(1, STEPS + 2, step_y, yp[pl.ds(base, BY), :], unroll=8)
        for after, tk, there in sides:
            @pl.when(there)
            def _():
                remote(
                    yo.at[turn], zb.at[2 * (1 - after), j], r3_send.at[2 * after], r3_recv.at[2 * (1 - after)],
                    (i, to, tk),
                )

        if turn < NJ - 1:
            remote(yo.at[turn], zb.at[1, j], r3_send.at[1], r3_recv.at[1], (i, to, k))
        else:
            pltpu.make_async_copy(yo.at[turn], zb.at[1, j], r3_recv.at[1]).start()

    drain(scb, sc_recv)
    for b in range(NI):
        score_ref[:, 8 * b : 8 * b + 8, :] = scb[b]
    drain(zb.at[1], r3_recv.at[1])
    for after, tk, there in sides:
        @pl.when(there)
        def _():
            drain(zb.at[2 * after], r3_recv.at[2 * after])


    for h in range(2):
        for d in range(3):
            turned = zb[d, 2 * h : 2 * h + 2].reshape(128, BZ).T
            if d == 0:
                turned = jnp.where(first_z, FAR, turned)
            if d == 2:
                turned = jnp.where(last_z, FAR, turned)
            tz[h, 128 * d : 128 * d + 128, :] = turned

        def step_z(n, acc):
            square = (n * n).astype(F32)
            low = tz[h, pl.ds(128 - n, 128), :]
            high = tz[h, pl.ds(128 + n, 128), :]
            return jnp.minimum(acc, jnp.minimum(low, high) + square)

        least = lax.fori_loop(1, STEPS + 2, step_z, tz[h, 128:256, :], unroll=4)
        depth_ref[2 * h : 2 * h + 2] = (least * (1.0 / RADIUS)).T.reshape(2, BY, BZ)

    seven = pl.ds(0, NI - 1)
    drain(mr.at[seven], m_send)
    drain(r1.at[seven], r1_send)
    drain(scb.at[seven], sc_send)
    drain(rows_in.at[pl.ds(0, 2)], row_send)
    drain(yb.at[pl.ds(0, NI * NJ - 1)], r2_send)
    drain(zb.at[1, pl.ds(0, NJ - 1)], r3_send.at[1])
    for after, tk, there in sides:
        @pl.when(there)
        def _():
            drain(rims_y.at[after, pl.ds(0, 2)], ry_send.at[after])
            drain(rims.at[after], t_send.at[after])
            drain(zb.at[2 * after], r3_send.at[2 * after])


def shards(features, conv_weight, mask):
    vmem = pl.BlockSpec(memory_space=pltpu.VMEM)
    hbm = pl.BlockSpec(memory_space=pltpu.HBM)
    tile = (8, BZ)
    dma = pltpu.SemaphoreType.DMA
    out = jax.ShapeDtypeStruct((BX, BY, BZ), F32)
    return pl.pallas_call(
        kernel,
        out_shape=(out, out),
        in_specs=[hbm] * 3,
        out_specs=(vmem, vmem),
        scratch_shapes=[
            pltpu.VMEM((32, BX, BY, BZ), jnp.bfloat16),
            pltpu.VMEM((27, 32), jnp.bfloat16),
            pltpu.VMEM((BX, BY, BZ), jnp.int32),
            pltpu.VMEM((288, 512), jnp.bfloat16),
            pltpu.VMEM((3, PLANES, BY + 16, BZ), F32),
            pltpu.VMEM((PLANES, BY + 16, BZ), F32),
            pltpu.VMEM((5, *tile), F32),
            pltpu.VMEM((NI, PLANES, *tile), F32),
            pltpu.VMEM((2, NI, *tile), F32),
            pltpu.VMEM((2, NI, *tile), F32),
            pltpu.VMEM((NI, *tile), F32),
            pltpu.VMEM((NI, BX, *tile), jnp.int32),
            pltpu.VMEM((32, *tile), F32),
            pltpu.VMEM((NI, BX, *tile), F32),
            pltpu.VMEM((32, *tile), F32),
            pltpu.VMEM((32, *tile), F32),
            pltpu.VMEM((32, *tile), F32),
            pltpu.VMEM((512, BZ), F32),
            pltpu.VMEM((NJ, BY, BZ), F32),
            pltpu.VMEM((3, NJ, BY, BZ), F32),
            pltpu.VMEM((2, 384, BZ), F32),
            dma((3,)),
        ] + [dma] * 10 + [dma((2,))] * 4 + [dma((3,))] * 2,
        compiler_params=pltpu.CompilerParams(
            collective_id=0, has_side_effects=True, vmem_limit_bytes=40 * 1024 * 1024
        ),
    )(features, conv_weight, mask)


def solution(mesh):
    in_specs = (P(None, "gx", "gy", "gz"), P(), P("gx", "gy", "gz"))
    out_specs = (P("gx", "gy", "gz"), P("gx", "gy", "gz"))
    return jax.shard_map(shards, mesh=mesh, in_specs=in_specs, out_specs=out_specs, check_vma=False)
```

```python
import functools

import jax
import jax.numpy as jnp
from jax import lax
from jax.experimental import pallas as pl
from jax.experimental.pallas import tpu as pltpu
from jax.sharding import PartitionSpec as P

MESH = pl.DeviceIdType.MESH
RADIUS = 128
CEILING = float(RADIUS * RADIUS)
FAR = 1.0e9
F32 = jnp.float32
BX, BY, BZ = 4, 64, 128
NI, NJ, NK = 8, 4, 8
PLANES = BX + 2
STEPS = RADIUS - 1


def iota(shape, axis):
    return lax.broadcasted_iota(jnp.int32, shape, axis)


def banded_weights(w_ref, wb_ref):
    rows, cols = 9 * 32, 32 * 16
    weights = w_ref[...]
    row = iota((rows, 27), 0)
    tap = iota((rows, 27), 1)
    group = row // 32
    spread = (iota((32, cols), 1) // 16 == iota((32, cols), 0)).astype(jnp.bfloat16)
    gap = iota((rows, cols), 1) % 16 - (iota((rows, cols), 0) % 32 - 8)
    total = jnp.zeros((rows, cols), F32)
    for b in range(3):
        pick = (tap == (group // 3) * 9 + 3 * b + group % 3).astype(jnp.bfloat16)
        own = jnp.dot(pick, weights, preferred_element_type=F32).astype(jnp.bfloat16)
        wide = jnp.dot(own, spread, preferred_element_type=F32)
        total = jnp.where(gap == b - 1, wide, total)
    wb_ref[...] = total.astype(jnp.bfloat16)


def kernel(
    f_hbm, w_hbm, m_hbm, score_ref, depth_ref,
    f_ref, w_ref, m_ref, wb, s3, s, pack, rim, r1, rims, rows_in, mr, sc, scb, xin, xo, yb, yp, yo, zb, tz,
    in_sems, m_send, m_recv, r1_send, r1_recv, row_send, row_recv, sc_send, sc_recv,
    r2_send, r2_recv, t_send, t_recv, r3_send, r3_recv,
):
    i, j, k = lax.axis_index("gx"), lax.axis_index("gy"), lax.axis_index("gz")
    loads = [
        pltpu.make_async_copy(source, target, in_sems.at[n])
        for n, (source, target) in enumerate(((w_hbm, w_ref), (f_hbm, f_ref), (m_hbm, m_ref)))
    ]
    for load in loads:
        load.start()

    def around(position, size):
        return [position] + [
            jnp.where(position >= size - d, position - (size - d), position + d) for d in range(1, size)
        ]

    xs_of, ys_of = around(i, NI), around(j, NJ)
    first_z, last_z = k == 0, k == NK - 1
    sides = ((1, k + 1, jnp.logical_not(last_z)), (0, k - 1, jnp.logical_not(first_z)))
    side_count = 2 - first_z.astype(jnp.int32) - last_z.astype(jnp.int32)

    barrier = pltpu.get_barrier_semaphore()

    def greet(*device):
        pl.semaphore_signal(barrier, inc=1, device_id=device, device_id_type=MESH)

    for _, tk, there in sides:
        @pl.when(there)
        def _():
            greet(i, j, tk)

    for ti in xs_of:
        for tj in ys_of:
            if ti is not i or tj is not j:
                greet(ti, tj, k)
    greeted = NI * NJ - 1 + side_count

    loads[0].wait()
    banded_weights(w_ref, wb)
    s3[...] = jnp.zeros_like(s3)
    loads[1].wait()

    def conv_block(q, carry):
        start = pl.multiple_of(q * 16, 16)
        for xs in range(BX):
            block = f_ref[:, xs, pl.ds(start, 16), :].reshape(32 * 16, BZ)
            part = jnp.dot(wb[...], block, preferred_element_type=F32)
            for a in range(3):
                for c in range(3):
                    at = (3 * a + c) * 32
                    s3[c, xs - a + 2, pl.ds(start, 32), :] += part[at : at + 32]
        return carry

    lax.fori_loop(0, BY // 16, conv_block, 0)

    lane = iota((8, BZ), 1)
    sub = iota((8, BZ), 0)
    edge = (lane == 0) | (lane == BZ - 1)
    zero = jnp.zeros((8, BZ), F32)
    pack[...] = jnp.zeros_like(pack)

    def shift_plane(p, tile):
        for t in range(10):
            rows = pl.ds(8 * t, 8)
            right = pltpu.roll(s3[0, p, rows, :], 1, 1)
            left = pltpu.roll(s3[2, p, rows, :], BZ - 1, 1)
            mine = s3[1, p, rows, :] + jnp.where(lane == 0, 0.0, right) + jnp.where(lane == BZ - 1, 0.0, left)
            s[p, rows, :] = mine
            outer = jnp.where(lane == 0, right, left)
            if t == 0:
                pack[1, pl.ds(p, 1), :] = mine[7:8]
                pack[2, pl.ds(p, 1), :] = outer[7:8]
            elif t == 9:
                pack[3, pl.ds(p, 1), :] = mine[0:1]
                pack[4, pl.ds(p, 1), :] = outer[0:1]
            else:
                v = 2 * (p * 8 + t - 1)
                moved = pltpu.roll(outer, v, 1)
                tile = jnp.where((lane == v) | (lane == (v + BZ - 1) % BZ), moved, tile)
        return tile

    tile = lax.fori_loop(0, PLANES, shift_plane, zero)
    for near, v in ((2, 96), (4, 98)):
        tile = jnp.where((lane == v) | (lane == v - 1), pltpu.roll(pack[near], v, 1), tile)
    rim[...] = tile
    at_end = (i == 0) | (i == NI - 1)
    far = jnp.full((128, BZ), FAR, F32)
    yp[0:128] = far
    yp[384:512] = far

    @pl.when(jnp.logical_not(at_end))
    def _():
        rows_in[...] = jnp.zeros_like(rows_in)

    loads[2].wait()
    pl.semaphore_wait(barrier, greeted)

    def remote(source, target, send, recv, device):
        pltpu.make_async_remote_copy(
            source, target, send, recv, device_id=device, device_id_type=MESH
        ).start()

    def drain(ref, semaphore):
        pltpu.make_async_copy(ref, ref, semaphore).wait()

    for after, tk, there in sides:
        @pl.when(there)
        def _():
            remote(rim, rims.at[1 - after], t_send.at[after], t_recv.at[1 - after], (i, j, tk))

    def mask_rows(to):
        return m_ref.at[:, pl.ds(pl.multiple_of(to * 8, 8), 8), :]

    for ti in xs_of[1:]:
        remote(mask_rows(ti), mr.at[i], m_send, m_recv, (ti, j, k))
    pltpu.make_async_copy(mask_rows(i), mr.at[i], m_recv).start()

    for after, tk, there in sides:
        @pl.when(there)
        def _():
            drain(rims.at[after], t_recv.at[after])

    both = jnp.where(lane % 2 == 0, jnp.where(first_z, zero, rims[0]), jnp.where(last_z, zero, rims[1]))
    for near, v in ((1, 96), (3, 98)):
        pack[near] += jnp.where(edge, pltpu.roll(both, BZ - v, 1), 0.0)

    def add_rims(p, turned):
        for t in range(8):
            rows = pl.ds(8 * t + 8, 8)
            moved = turned if t == 0 else pltpu.roll(turned, BZ - 2 * t, 1)
            s[p, rows, :] += jnp.where(edge, moved, 0.0)
        return pltpu.roll(turned, BZ - 16, 1)

    lax.fori_loop(0, PLANES, add_rims, both)

    def part_rows(to):
        return s.at[:, pl.ds(pl.multiple_of(8 + to * 8, 8), 8), :]

    for ti in xs_of[1:]:
        remote(part_rows(ti), r1.at[i], r1_send, r1_recv, (ti, j, k))
    for ti, tj, near in ((NI - 1, ys_of[NJ - 1], 1), (0, ys_of[1], 3)):
        remote(pack.at[near], rows_in.at[i], row_send, row_recv, (ti, tj, k))
    pltpu.make_async_copy(part_rows(i), r1.at[i], r1_recv).start()
    outside = ((i == 0) & (j == 0)) | ((i == NI - 1) & (j == NJ - 1))

    @pl.when(at_end)
    def _():
        drain(rows_in, row_recv)

    drain(r1, r1_recv)
    drain(mr, m_recv)

    end_row = sub == jnp.where(i == 0, 0, 7)
    parts = []
    for b in range(NI):
        rows = rows_in[b]
        rows = jnp.where(outside, zero, rows)
        planes = []
        for p in range(PLANES):
            planes.append(
                r1[b, p]
                + jnp.where(end_row, jnp.broadcast_to(rows[p : p + 1], (8, BZ)), 0.0)
            )
        parts.append(planes)
    for b in range(NI):
        for a in range(BX):
            value = parts[b][a + 1]
            if a == 0 and b > 0:
                value += parts[b - 1][BX + 1]
            if a == BX - 1 and b < NI - 1:
                value += parts[b + 1][0]
            x = BX * b + a
            sc[x] = value
            cost = CEILING / (1.0 + jnp.exp(-value))
            xin[x] = jnp.where(mr[b, a] == 1, CEILING, cost)

    acc = xin[...]
    for n in range(1, 32):
        square = float(n * n)
        if n < 16:
            pair = jnp.minimum(xin[0 : 32 - 2 * n], xin[2 * n : 32]) + square
            least = jnp.concatenate([xin[n : 2 * n] + square, pair, xin[32 - 2 * n : 32 - n] + square], axis=0)
            acc = jnp.minimum(acc, least)
        else:
            low = jnp.minimum(acc[0 : 32 - n], xin[n:32] + square)
            high = jnp.minimum(acc[n:32], xin[0 : 32 - n] + square)
            middle = [acc[32 - n : n]] if n > 16 else []
            acc = jnp.concatenate([low, *middle, high], axis=0)
    xo[...] = acc

    for ti in xs_of:
        for tj in ys_of:
            if ti is not i or tj is not j:
                remote(xo.at[ti * NJ + tj], yb.at[j * NI + i], r2_send, r2_recv, (ti, tj, k))
    pltpu.make_async_copy(xo.at[i * NJ + j], yb.at[j * NI + i], r2_recv).start()

    for ti in xs_of[1:]:
        remote(sc.at[pl.ds(ti * BX, BX)], scb.at[i], sc_send, sc_recv, (ti, j, k))
    pltpu.make_async_copy(sc.at[pl.ds(i * BX, BX)], scb.at[i], sc_recv).start()

    drain(yb, r2_recv)
    yp[128:384] = yb[...].reshape(256, BZ)

    for turn, to in enumerate((ys_of[2], NJ - 1 - j, NJ - 1 - ys_of[2], j)):
        base = pl.multiple_of(128 + to * BY, BY)
        far_chip = 1 if turn < 2 else 0

        def step_y(n, acc):
            square = (n * n).astype(F32)
            low = yp[pl.ds(base - n, BY), :]
            high = yp[pl.ds(base + n, BY), :]
            return jnp.minimum(acc, jnp.minimum(low, high) + square)

        yo[turn] = lax.fori_loop(1, STEPS + 2, step_y, yp[pl.ds(base, BY), :], unroll=8)
        for after, tk, there in sides:
            @pl.when(there)
            def _():
                remote(
                    yo.at[turn], zb.at[2 * (1 - after), j], r3_send.at[2 * after],
                    r3_recv.at[2 * (1 - after), far_chip],
                    (i, to, tk),
                )

        if turn < NJ - 1:
            remote(yo.at[turn], zb.at[1, j], r3_send.at[1], r3_recv.at[1, far_chip], (i, to, k))
        else:
            pltpu.make_async_copy(yo.at[turn], zb.at[1, j], r3_recv.at[1, far_chip]).start()

    drain(scb, sc_recv)
    for b in range(NI):
        score_ref[:, 8 * b : 8 * b + 8, :] = scb[b]
    own_pair = jnp.where(j >= 2, 2, 0)
    for h, pair in enumerate((own_pair, 2 - own_pair)):
        two = pl.ds(pair, 2)
        drain(zb.at[1, two], r3_recv.at[1, h])
        for after, tk, there in sides:
            @pl.when(there)
            def _():
                drain(zb.at[2 * after, two], r3_recv.at[2 * after, h])

        for d in range(3):
            turned = zb[d, two].reshape(128, BZ).T
            if d == 0:
                turned = jnp.where(first_z, FAR, turned)
            if d == 2:
                turned = jnp.where(last_z, FAR, turned)
            tz[h, 128 * d : 128 * d + 128, :] = turned

        def step_z(n, acc):
            square = (n * n).astype(F32)
            low = tz[h, pl.ds(128 - n, 128), :]
            high = tz[h, pl.ds(128 + n, 128), :]
            return jnp.minimum(acc, jnp.minimum(low, high) + square)

        least = lax.fori_loop(1, STEPS + 2, step_z, tz[h, 128:256, :], unroll=4)
        depth_ref[two] = (least * (1.0 / RADIUS)).T.reshape(2, BY, BZ)

    seven = pl.ds(0, NI - 1)
    drain(mr.at[seven], m_send)
    drain(r1.at[seven], r1_send)
    drain(scb.at[seven], sc_send)
    drain(rows_in.at[pl.ds(0, 2)], row_send)
    drain(yb.at[pl.ds(0, NI * NJ - 1)], r2_send)
    drain(zb.at[1, pl.ds(0, NJ - 1)], r3_send.at[1])
    for after, tk, there in sides:
        @pl.when(there)
        def _():
            drain(rims.at[after], t_send.at[after])
            drain(zb.at[2 * after], r3_send.at[2 * after])


def shards(features, conv_weight, mask):
    vmem = pl.BlockSpec(memory_space=pltpu.VMEM)
    hbm = pl.BlockSpec(memory_space=pltpu.HBM)
    tile = (8, BZ)
    dma = pltpu.SemaphoreType.DMA
    out = jax.ShapeDtypeStruct((BX, BY, BZ), F32)
    return pl.pallas_call(
        kernel,
        out_shape=(out, out),
        in_specs=[hbm] * 3,
        out_specs=(vmem, vmem),
        scratch_shapes=[
            pltpu.VMEM((32, BX, BY, BZ), jnp.bfloat16),
            pltpu.VMEM((27, 32), jnp.bfloat16),
            pltpu.VMEM((BX, BY, BZ), jnp.int32),
            pltpu.VMEM((288, 512), jnp.bfloat16),
            pltpu.VMEM((3, PLANES, BY + 16, BZ), F32),
            pltpu.VMEM((PLANES, BY + 16, BZ), F32),
            pltpu.VMEM((5, *tile), F32),
            pltpu.VMEM(tile, F32),
            pltpu.VMEM((NI, PLANES, *tile), F32),
            pltpu.VMEM((2, *tile), F32),
            pltpu.VMEM((NI, *tile), F32),
            pltpu.VMEM((NI, BX, *tile), jnp.int32),
            pltpu.VMEM((32, *tile), F32),
            pltpu.VMEM((NI, BX, *tile), F32),
            pltpu.VMEM((32, *tile), F32),
            pltpu.VMEM((32, *tile), F32),
            pltpu.VMEM((32, *tile), F32),
            pltpu.VMEM((512, BZ), F32),
            pltpu.VMEM((NJ, BY, BZ), F32),
            pltpu.VMEM((3, NJ, BY, BZ), F32),
            pltpu.VMEM((2, 384, BZ), F32),
            dma((3,)),
        ] + [dma] * 10 + [dma((2,))] * 2 + [dma((3,)), dma((3, 2))],
        compiler_params=pltpu.CompilerParams(
            collective_id=0, has_side_effects=True, vmem_limit_bytes=40 * 1024 * 1024
        ),
    )(features, conv_weight, mask)


def solution(mesh):
    in_specs = (P(None, "gx", "gy", "gz"), P(), P("gx", "gy", "gz"))
    out_specs = (P("gx", "gy", "gz"), P("gx", "gy", "gz"))
    return jax.shard_map(shards, mesh=mesh, in_specs=in_specs, out_specs=out_specs, check_vma=False)
```

```python
import functools

import jax
import jax.numpy as jnp
from jax import lax
from jax.experimental import pallas as pl
from jax.experimental.pallas import tpu as pltpu
from jax.sharding import PartitionSpec as P

MESH = pl.DeviceIdType.MESH
RADIUS = 128
CEILING = float(RADIUS * RADIUS)
FAR = 1.0e9
F32 = jnp.float32
BX, BY, BZ = 4, 64, 128
NI, NJ, NK = 8, 4, 8
PLANES = BX + 2
STEPS = RADIUS - 1


def iota(shape, axis):
    return lax.broadcasted_iota(jnp.int32, shape, axis)


def banded_weights(w_ref, wb_ref):
    rows, cols = 9 * 32, 32 * 16
    weights = w_ref[...]
    row = iota((rows, 27), 0)
    tap = iota((rows, 27), 1)
    group = row // 32
    spread = (iota((32, cols), 1) // 16 == iota((32, cols), 0)).astype(jnp.bfloat16)
    gap = iota((rows, cols), 1) % 16 - (iota((rows, cols), 0) % 32 - 8)
    total = jnp.zeros((rows, cols), F32)
    for b in range(3):
        pick = (tap == (group // 3) * 9 + 3 * b + group % 3).astype(jnp.bfloat16)
        own = jnp.dot(pick, weights, preferred_element_type=F32).astype(jnp.bfloat16)
        wide = jnp.dot(own, spread, preferred_element_type=F32)
        total = jnp.where(gap == b - 1, wide, total)
    wb_ref[...] = total.astype(jnp.bfloat16)


def kernel(
    f_hbm, w_hbm, m_hbm, score_ref, least_ref,
    f_ref, w_ref, m_ref, wb, s3, s, pack, rim, r1, rims, rows_in, mr, sc, scb, xin, xo, yb, yp, yo, zb, tz,
    in_sems, m_send, m_recv, r1_send, r1_recv, row_send, row_recv, sc_send, sc_recv,
    r2_send, r2_recv, t_send, t_recv, r3_send, r3_recv,
):
    i, j, k = lax.axis_index("gx"), lax.axis_index("gy"), lax.axis_index("gz")
    loads = [
        pltpu.make_async_copy(source, target, in_sems.at[n])
        for n, (source, target) in enumerate(((w_hbm, w_ref), (f_hbm, f_ref), (m_hbm, m_ref)))
    ]
    for load in loads:
        load.start()

    def around(position, size):
        return [position] + [
            jnp.where(position >= size - d, position - (size - d), position + d) for d in range(1, size)
        ]

    xs_of, ys_of = around(i, NI), around(j, NJ)
    first_z, last_z = k == 0, k == NK - 1
    sides = ((1, k + 1, jnp.logical_not(last_z)), (0, k - 1, jnp.logical_not(first_z)))
    side_count = 2 - first_z.astype(jnp.int32) - last_z.astype(jnp.int32)

    barrier = pltpu.get_barrier_semaphore()

    def greet(*device):
        pl.semaphore_signal(barrier, inc=1, device_id=device, device_id_type=MESH)

    for _, tk, there in sides:
        @pl.when(there)
        def _():
            greet(i, j, tk)

    for ti in xs_of:
        for tj in ys_of:
            if ti is not i or tj is not j:
                greet(ti, tj, k)
    greeted = NI * NJ - 1 + side_count

    loads[0].wait()
    banded_weights(w_ref, wb)
    s3[...] = jnp.zeros_like(s3)
    loads[1].wait()

    def conv_block(q, carry):
        start = pl.multiple_of(q * 16, 16)
        for xs in range(BX):
            block = f_ref[:, xs, pl.ds(start, 16), :].reshape(32 * 16, BZ)
            part = jnp.dot(wb[...], block, preferred_element_type=F32)
            for a in range(3):
                for c in range(3):
                    at = (3 * a + c) * 32
                    s3[c, xs - a + 2, pl.ds(start, 32), :] += part[at : at + 32]
        return carry

    lax.fori_loop(0, BY // 16, conv_block, 0)

    lane = iota((8, BZ), 1)
    sub = iota((8, BZ), 0)
    edge = (lane == 0) | (lane == BZ - 1)
    zero = jnp.zeros((8, BZ), F32)
    pack[...] = jnp.zeros_like(pack)

    def shift_plane(p, tile):
        for t in range(10):
            rows = pl.ds(8 * t, 8)
            right = pltpu.roll(s3[0, p, rows, :], 1, 1)
            left = pltpu.roll(s3[2, p, rows, :], BZ - 1, 1)
            mine = s3[1, p, rows, :] + jnp.where(lane == 0, 0.0, right) + jnp.where(lane == BZ - 1, 0.0, left)
            s[p, rows, :] = mine
            outer = jnp.where(lane == 0, right, left)
            if t == 0:
                pack[1, pl.ds(p, 1), :] = mine[7:8]
                pack[2, pl.ds(p, 1), :] = outer[7:8]
            elif t == 9:
                pack[3, pl.ds(p, 1), :] = mine[0:1]
                pack[4, pl.ds(p, 1), :] = outer[0:1]
            else:
                v = 2 * (p * 8 + t - 1)
                moved = pltpu.roll(outer, v, 1)
                tile = jnp.where((lane == v) | (lane == (v + BZ - 1) % BZ), moved, tile)
        return tile

    tile = lax.fori_loop(0, PLANES, shift_plane, zero)
    for near, v in ((2, 96), (4, 98)):
        tile = jnp.where((lane == v) | (lane == v - 1), pltpu.roll(pack[near], v, 1), tile)
    rim[...] = tile
    at_end = (i == 0) | (i == NI - 1)
    far = jnp.full((128, BZ), FAR, F32)
    yp[0:128] = far
    yp[384:512] = far

    @pl.when(jnp.logical_not(at_end))
    def _():
        rows_in[...] = jnp.zeros_like(rows_in)

    loads[2].wait()
    pl.semaphore_wait(barrier, greeted)

    def remote(source, target, send, recv, device):
        pltpu.make_async_remote_copy(
            source, target, send, recv, device_id=device, device_id_type=MESH
        ).start()

    def drain(ref, semaphore):
        pltpu.make_async_copy(ref, ref, semaphore).wait()

    for after, tk, there in sides:
        @pl.when(there)
        def _():
            remote(rim, rims.at[1 - after], t_send.at[after], t_recv.at[1 - after], (i, j, tk))

    def mask_rows(to):
        return m_ref.at[:, pl.ds(pl.multiple_of(to * 8, 8), 8), :]

    for ti in xs_of[1:]:
        remote(mask_rows(ti), mr.at[i], m_send, m_recv, (ti, j, k))
    pltpu.make_async_copy(mask_rows(i), mr.at[i], m_recv).start()

    for after, tk, there in sides:
        @pl.when(there)
        def _():
            drain(rims.at[after], t_recv.at[after])

    both = jnp.where(lane % 2 == 0, jnp.where(first_z, zero, rims[0]), jnp.where(last_z, zero, rims[1]))
    for near, v in ((1, 96), (3, 98)):
        pack[near] += jnp.where(edge, pltpu.roll(both, BZ - v, 1), 0.0)

    def add_rims(p, turned):
        for t in range(8):
            rows = pl.ds(8 * t + 8, 8)
            moved = turned if t == 0 else pltpu.roll(turned, BZ - 2 * t, 1)
            s[p, rows, :] += jnp.where(edge, moved, 0.0)
        return pltpu.roll(turned, BZ - 16, 1)

    lax.fori_loop(0, PLANES, add_rims, both)

    def part_rows(to):
        return s.at[:, pl.ds(pl.multiple_of(8 + to * 8, 8), 8), :]

    for ti in xs_of[1:]:
        remote(part_rows(ti), r1.at[i], r1_send, r1_recv, (ti, j, k))
    for ti, tj, near in ((NI - 1, ys_of[NJ - 1], 1), (0, ys_of[1], 3)):
        remote(pack.at[near], rows_in.at[i], row_send, row_recv, (ti, tj, k))
    pltpu.make_async_copy(part_rows(i), r1.at[i], r1_recv).start()
    outside = ((i == 0) & (j == 0)) | ((i == NI - 1) & (j == NJ - 1))

    @pl.when(at_end)
    def _():
        drain(rows_in, row_recv)

    drain(r1, r1_recv)
    drain(mr, m_recv)

    end_row = sub == jnp.where(i == 0, 0, 7)
    parts = []
    for b in range(NI):
        rows = rows_in[b]
        rows = jnp.where(outside, zero, rows)
        planes = []
        for p in range(PLANES):
            planes.append(
                r1[b, p]
                + jnp.where(end_row, jnp.broadcast_to(rows[p : p + 1], (8, BZ)), 0.0)
            )
        parts.append(planes)
    for b in range(NI):
        for a in range(BX):
            value = parts[b][a + 1]
            if a == 0 and b > 0:
                value += parts[b - 1][BX + 1]
            if a == BX - 1 and b < NI - 1:
                value += parts[b + 1][0]
            x = BX * b + a
            sc[x] = value
            cost = CEILING / (1.0 + jnp.exp(-value))
            xin[x] = jnp.where(mr[b, a] == 1, CEILING, cost)

    acc = xin[...]
    for n in range(1, 32):
        square = float(n * n)
        if n < 16:
            pair = jnp.minimum(xin[0 : 32 - 2 * n], xin[2 * n : 32]) + square
            least = jnp.concatenate([xin[n : 2 * n] + square, pair, xin[32 - 2 * n : 32 - n] + square], axis=0)
            acc = jnp.minimum(acc, least)
        else:
            low = jnp.minimum(acc[0 : 32 - n], xin[n:32] + square)
            high = jnp.minimum(acc[n:32], xin[0 : 32 - n] + square)
            middle = [acc[32 - n : n]] if n > 16 else []
            acc = jnp.concatenate([low, *middle, high], axis=0)
    xo[...] = acc

    for ti in xs_of:
        for tj in ys_of:
            if ti is not i or tj is not j:
                remote(xo.at[ti * NJ + tj], yb.at[j * NI + i], r2_send, r2_recv, (ti, tj, k))
    pltpu.make_async_copy(xo.at[i * NJ + j], yb.at[j * NI + i], r2_recv).start()

    for ti in xs_of[1:]:
        remote(sc.at[pl.ds(ti * BX, BX)], scb.at[i], sc_send, sc_recv, (ti, j, k))
    pltpu.make_async_copy(sc.at[pl.ds(i * BX, BX)], scb.at[i], sc_recv).start()

    drain(yb, r2_recv)
    yp[128:384] = yb[...].reshape(256, BZ)

    for turn, to in enumerate((ys_of[2], NJ - 1 - j, NJ - 1 - ys_of[2], j)):
        base = pl.multiple_of(128 + to * BY, BY)
        far_chip = 1 if turn < 2 else 0

        def step_y(n, acc):
            square = (n * n).astype(F32)
            low = yp[pl.ds(base - n, BY), :]
            high = yp[pl.ds(base + n, BY), :]
            return jnp.minimum(acc, jnp.minimum(low, high) + square)

        yo[turn] = lax.fori_loop(1, STEPS + 2, step_y, yp[pl.ds(base, BY), :], unroll=8)
        for after, tk, there in sides:
            @pl.when(there)
            def _():
                remote(
                    yo.at[turn], zb.at[2 * (1 - after), j], r3_send.at[2 * after],
                    r3_recv.at[2 * (1 - after), far_chip],
                    (i, to, tk),
                )

        if turn < NJ - 1:
            remote(yo.at[turn], zb.at[1, j], r3_send.at[1], r3_recv.at[1, far_chip], (i, to, k))
        else:
            pltpu.make_async_copy(yo.at[turn], zb.at[1, j], r3_recv.at[1, far_chip]).start()

    drain(scb, sc_recv)
    for b in range(NI):
        score_ref[:, 8 * b : 8 * b + 8, :] = scb[b]
    own_pair = jnp.where(j >= 2, 2, 0)
    for h, pair in enumerate((own_pair, 2 - own_pair)):
        two = pl.ds(pair, 2)
        drain(zb.at[1, two], r3_recv.at[1, h])
        for after, tk, there in sides:
            @pl.when(there)
            def _():
                drain(zb.at[2 * after, two], r3_recv.at[2 * after, h])

        for d in range(3):
            turned = zb[d, two].reshape(128, BZ).T
            if d == 0:
                turned = jnp.where(first_z, FAR, turned)
            if d == 2:
                turned = jnp.where(last_z, FAR, turned)
            tz[h, 128 * d : 128 * d + 128, :] = turned

        def step_z(n, acc):
            square = (n * n).astype(F32)
            low = tz[h, pl.ds(128 - n, 128), :]
            high = tz[h, pl.ds(128 + n, 128), :]
            return jnp.minimum(acc, jnp.minimum(low, high) + square)

        first = jnp.where(pair == 0, 0, 1)
        least_ref[first] = lax.fori_loop(1, STEPS + 2, step_z, tz[h, 128:256, :], unroll=4)

    seven = pl.ds(0, NI - 1)
    drain(mr.at[seven], m_send)
    drain(r1.at[seven], r1_send)
    drain(scb.at[seven], sc_send)
    drain(rows_in.at[pl.ds(0, 2)], row_send)
    drain(yb.at[pl.ds(0, NI * NJ - 1)], r2_send)
    drain(zb.at[1, pl.ds(0, NJ - 1)], r3_send.at[1])
    for after, tk, there in sides:
        @pl.when(there)
        def _():
            drain(rims.at[after], t_send.at[after])
            drain(zb.at[2 * after], r3_send.at[2 * after])


def finish(score_in, least_ref, score_hbm, depth_hbm, depth, sems):
    copies = [pltpu.make_async_copy(score_in, score_hbm, sems.at[2])]
    copies[0].start()
    for h in range(2):
        planes = pl.ds(2 * h, 2)
        depth[planes] = (least_ref[h] * (1.0 / RADIUS)).T.reshape(2, BY, BZ)
        copies.append(pltpu.make_async_copy(depth.at[planes], depth_hbm.at[planes], sems.at[h]))
        copies[-1].start()
    for copy in copies:
        copy.wait()


def shards(features, conv_weight, mask):
    vmem = pl.BlockSpec(memory_space=pltpu.VMEM)
    hbm = pl.BlockSpec(memory_space=pltpu.HBM)
    tile = (8, BZ)
    dma = pltpu.SemaphoreType.DMA
    out = jax.ShapeDtypeStruct((BX, BY, BZ), F32)
    score, least = pl.pallas_call(
        kernel,
        out_shape=(out, jax.ShapeDtypeStruct((2, 128, BZ), F32)),
        in_specs=[hbm] * 3,
        out_specs=(vmem, vmem),
        scratch_shapes=[
            pltpu.VMEM((32, BX, BY, BZ), jnp.bfloat16),
            pltpu.VMEM((27, 32), jnp.bfloat16),
            pltpu.VMEM((BX, BY, BZ), jnp.int32),
            pltpu.VMEM((288, 512), jnp.bfloat16),
            pltpu.VMEM((3, PLANES, BY + 16, BZ), F32),
            pltpu.VMEM((PLANES, BY + 16, BZ), F32),
            pltpu.VMEM((5, *tile), F32),
            pltpu.VMEM(tile, F32),
            pltpu.VMEM((NI, PLANES, *tile), F32),
            pltpu.VMEM((2, *tile), F32),
            pltpu.VMEM((NI, *tile), F32),
            pltpu.VMEM((NI, BX, *tile), jnp.int32),
            pltpu.VMEM((32, *tile), F32),
            pltpu.VMEM((NI, BX, *tile), F32),
            pltpu.VMEM((32, *tile), F32),
            pltpu.VMEM((32, *tile), F32),
            pltpu.VMEM((32, *tile), F32),
            pltpu.VMEM((512, BZ), F32),
            pltpu.VMEM((NJ, BY, BZ), F32),
            pltpu.VMEM((3, NJ, BY, BZ), F32),
            pltpu.VMEM((2, 384, BZ), F32),
            dma((3,)),
        ] + [dma] * 10 + [dma((2,))] * 2 + [dma((3,)), dma((3, 2))],
        compiler_params=pltpu.CompilerParams(
            collective_id=0, has_side_effects=True, vmem_limit_bytes=40 * 1024 * 1024
        ),
    )(*[pltpu.with_memory_space_constraint(x, pltpu.HBM) for x in (features, conv_weight, mask)])
    return pl.pallas_call(
        finish,
        out_shape=(out, out),
        in_specs=[vmem] * 2,
        out_specs=(hbm, hbm),
        scratch_shapes=[pltpu.VMEM((BX, BY, BZ), F32), dma((3,))],
        compiler_params=pltpu.CompilerParams(vmem_limit_bytes=2 * 1024 * 1024),
    )(score, least)


def solution(mesh):
    in_specs = (P(None, "gx", "gy", "gz"), P(), P("gx", "gy", "gz"))
    out_specs = (P("gx", "gy", "gz"), P("gx", "gy", "gz"))
    return jax.shard_map(shards, mesh=mesh, in_specs=in_specs, out_specs=out_specs, check_vma=False)
```

```python
import functools

import jax
import jax.numpy as jnp
from jax import lax
from jax.experimental import pallas as pl
from jax.experimental.pallas import tpu as pltpu
from jax.sharding import PartitionSpec as P

MESH = pl.DeviceIdType.MESH
RADIUS = 128
CEILING = float(RADIUS * RADIUS)
FAR = 1.0e9
F32 = jnp.float32
BX, BY, BZ = 4, 64, 128
NI, NJ, NK = 8, 4, 8
PLANES = BX + 2
STEPS = RADIUS - 1


def iota(shape, axis):
    return lax.broadcasted_iota(jnp.int32, shape, axis)


def banded_weights(w_ref, wb_ref):
    rows, cols = 9 * 32, 32 * 16
    weights = w_ref[...]
    row = iota((rows, 27), 0)
    tap = iota((rows, 27), 1)
    group = row // 32
    spread = (iota((32, cols), 1) // 16 == iota((32, cols), 0)).astype(jnp.bfloat16)
    gap = iota((rows, cols), 1) % 16 - (iota((rows, cols), 0) % 32 - 8)
    total = jnp.zeros((rows, cols), F32)
    for b in range(3):
        pick = (tap == (group // 3) * 9 + 3 * b + group % 3).astype(jnp.bfloat16)
        own = jnp.dot(pick, weights, preferred_element_type=F32).astype(jnp.bfloat16)
        wide = jnp.dot(own, spread, preferred_element_type=F32)
        total = jnp.where(gap == b - 1, wide, total)
    wb_ref[...] = total.astype(jnp.bfloat16)


def kernel(
    f_hbm, w_hbm, m_hbm, score_ref, least_ref,
    f_ref, w_ref, m_ref, wb, s3, s, pack, rim, r1, rims, rows_in, mr, sc, scb, xin, xo, yb, yp, yo, zb, tz,
    in_sems, m_send, m_recv, r1_send, r1_recv, row_send, row_recv, sc_send, sc_recv,
    r2_send, r2_recv, t_send, t_recv, r3_send, r3_recv,
):
    i, j, k = lax.axis_index("gx"), lax.axis_index("gy"), lax.axis_index("gz")
    loads = [
        pltpu.make_async_copy(source, target, in_sems.at[n])
        for n, (source, target) in enumerate(((w_hbm, w_ref), (f_hbm, f_ref), (m_hbm, m_ref)))
    ]
    for load in loads:
        load.start()

    def around(position, size):
        return [position] + [
            jnp.where(position >= size - d, position - (size - d), position + d) for d in range(1, size)
        ]

    xs_of, ys_of = around(i, NI), around(j, NJ)
    xs_of = [xs_of[d] for d in (0, 3, 5, 4, 1, 7, 2, 6)]
    ys_far = [ys_of[d] for d in (2, 3, 1, 0)]
    first_z, last_z = k == 0, k == NK - 1
    sides = ((1, k + 1, jnp.logical_not(last_z)), (0, k - 1, jnp.logical_not(first_z)))
    side_count = 2 - first_z.astype(jnp.int32) - last_z.astype(jnp.int32)

    barrier = pltpu.get_barrier_semaphore()

    def greet(*device):
        pl.semaphore_signal(barrier, inc=1, device_id=device, device_id_type=MESH)

    for _, tk, there in sides:
        @pl.when(there)
        def _():
            greet(i, j, tk)

    for ti in xs_of[1:] + [i]:
        for tj in ys_far:
            if ti is not i or tj is not j:
                greet(ti, tj, k)
    greeted = NI * NJ - 1 + side_count

    loads[0].wait()
    banded_weights(w_ref, wb)
    s3[...] = jnp.zeros_like(s3)
    loads[1].wait()

    def conv_block(q, carry):
        start = pl.multiple_of(q * 16, 16)
        for xs in range(BX):
            block = f_ref[:, xs, pl.ds(start, 16), :].reshape(32 * 16, BZ)
            part = jnp.dot(wb[...], block, preferred_element_type=F32)
            for a in range(3):
                for c in range(3):
                    at = (3 * a + c) * 32
                    s3[c, xs - a + 2, pl.ds(start, 32), :] += part[at : at + 32]
        return carry

    lax.fori_loop(0, BY // 16, conv_block, 0)

    lane = iota((8, BZ), 1)
    sub = iota((8, BZ), 0)
    edge = (lane == 0) | (lane == BZ - 1)
    zero = jnp.zeros((8, BZ), F32)
    pack[...] = jnp.zeros_like(pack)

    def shift_plane(p, tile):
        for t in range(10):
            rows = pl.ds(8 * t, 8)
            right = pltpu.roll(s3[0, p, rows, :], 1, 1)
            left = pltpu.roll(s3[2, p, rows, :], BZ - 1, 1)
            mine = s3[1, p, rows, :] + jnp.where(lane == 0, 0.0, right) + jnp.where(lane == BZ - 1, 0.0, left)
            s[p, rows, :] = mine
            outer = jnp.where(lane == 0, right, left)
            if t == 0:
                pack[1, pl.ds(p, 1), :] = mine[7:8]
                pack[2, pl.ds(p, 1), :] = outer[7:8]
            elif t == 9:
                pack[3, pl.ds(p, 1), :] = mine[0:1]
                pack[4, pl.ds(p, 1), :] = outer[0:1]
            else:
                v = 2 * (p * 8 + t - 1)
                moved = pltpu.roll(outer, v, 1)
                tile = jnp.where((lane == v) | (lane == (v + BZ - 1) % BZ), moved, tile)
        return tile

    tile = lax.fori_loop(0, PLANES, shift_plane, zero)
    for near, v in ((2, 96), (4, 98)):
        tile = jnp.where((lane == v) | (lane == v - 1), pltpu.roll(pack[near], v, 1), tile)
    rim[...] = tile
    at_end = (i == 0) | (i == NI - 1)
    far = jnp.full((128, BZ), FAR, F32)
    yp[0:128] = far
    yp[384:512] = far
    for h in range(2):
        tz[h, 0:128] = far
        tz[h, 256:384] = far

    @pl.when(jnp.logical_not(at_end))
    def _():
        rows_in[...] = jnp.zeros_like(rows_in)

    loads[2].wait()
    pl.semaphore_wait(barrier, greeted)

    def remote(source, target, send, recv, device):
        pltpu.make_async_remote_copy(
            source, target, send, recv, device_id=device, device_id_type=MESH
        ).start()

    def drain(ref, semaphore):
        pltpu.make_async_copy(ref, ref, semaphore).wait()

    for after, tk, there in sides:
        @pl.when(there)
        def _():
            remote(rim, rims.at[1 - after], t_send.at[after], t_recv.at[1 - after], (i, j, tk))

    def mask_rows(to):
        return m_ref.at[:, pl.ds(pl.multiple_of(to * 8, 8), 8), :]

    for ti in xs_of[1:]:
        remote(mask_rows(ti), mr.at[i], m_send, m_recv, (ti, j, k))
    pltpu.make_async_copy(mask_rows(i), mr.at[i], m_recv).start()

    for after, tk, there in sides:
        @pl.when(there)
        def _():
            drain(rims.at[after], t_recv.at[after])

    both = jnp.where(lane % 2 == 0, jnp.where(first_z, zero, rims[0]), jnp.where(last_z, zero, rims[1]))
    for near, v in ((1, 96), (3, 98)):
        pack[near] += jnp.where(edge, pltpu.roll(both, BZ - v, 1), 0.0)

    def add_rims(p, turned):
        for t in range(8):
            rows = pl.ds(8 * t + 8, 8)
            moved = turned if t == 0 else pltpu.roll(turned, BZ - 2 * t, 1)
            s[p, rows, :] += jnp.where(edge, moved, 0.0)
        return pltpu.roll(turned, BZ - 16, 1)

    lax.fori_loop(0, PLANES, add_rims, both)

    def part_rows(to):
        return s.at[:, pl.ds(pl.multiple_of(8 + to * 8, 8), 8), :]

    for ti in xs_of[1:]:
        remote(part_rows(ti), r1.at[i], r1_send, r1_recv, (ti, j, k))
    for ti, tj, near in ((NI - 1, ys_of[NJ - 1], 1), (0, ys_of[1], 3)):
        remote(pack.at[near], rows_in.at[i], row_send, row_recv, (ti, tj, k))
    pltpu.make_async_copy(part_rows(i), r1.at[i], r1_recv).start()
    outside = ((i == 0) & (j == 0)) | ((i == NI - 1) & (j == NJ - 1))

    @pl.when(at_end)
    def _():
        drain(rows_in, row_recv)

    drain(r1, r1_recv)
    drain(mr, m_recv)

    end_row = sub == jnp.where(i == 0, 0, 7)
    parts = []
    for b in range(NI):
        rows = rows_in[b]
        rows = jnp.where(outside, zero, rows)
        planes = []
        for p in range(PLANES):
            planes.append(
                r1[b, p]
                + jnp.where(end_row, jnp.broadcast_to(rows[p : p + 1], (8, BZ)), 0.0)
            )
        parts.append(planes)
    for b in range(NI):
        for a in range(BX):
            value = parts[b][a + 1]
            if a == 0 and b > 0:
                value += parts[b - 1][BX + 1]
            if a == BX - 1 and b < NI - 1:
                value += parts[b + 1][0]
            x = BX * b + a
            sc[x] = value
            cost = CEILING / (1.0 + jnp.exp(-value))
            xin[x] = jnp.where(mr[b, a] == 1, CEILING, cost)

    acc = xin[...]
    for n in range(1, 32):
        square = float(n * n)
        if n < 16:
            pair = jnp.minimum(xin[0 : 32 - 2 * n], xin[2 * n : 32]) + square
            least = jnp.concatenate([xin[n : 2 * n] + square, pair, xin[32 - 2 * n : 32 - n] + square], axis=0)
            acc = jnp.minimum(acc, least)
        else:
            low = jnp.minimum(acc[0 : 32 - n], xin[n:32] + square)
            high = jnp.minimum(acc[n:32], xin[0 : 32 - n] + square)
            middle = [acc[32 - n : n]] if n > 16 else []
            acc = jnp.concatenate([low, *middle, high], axis=0)
    xo[...] = acc

    for ti in xs_of[1:] + [i]:
        for tj in ys_far:
            if ti is not i or tj is not j:
                remote(xo.at[ti * NJ + tj], yb.at[j * NI + i], r2_send, r2_recv, (ti, tj, k))
    pltpu.make_async_copy(xo.at[i * NJ + j], yb.at[j * NI + i], r2_recv).start()

    for ti in xs_of[1:]:
        remote(sc.at[pl.ds(ti * BX, BX)], scb.at[i], sc_send, sc_recv, (ti, j, k))
    pltpu.make_async_copy(sc.at[pl.ds(i * BX, BX)], scb.at[i], sc_recv).start()

    drain(yb, r2_recv)
    yp[128:384] = yb[...].reshape(256, BZ)

    for turn, to in enumerate((ys_of[2], NJ - 1 - j, NJ - 1 - ys_of[2], j)):
        base = pl.multiple_of(128 + to * BY, BY)
        far_chip = 1 if turn < 2 else 0

        def step_y(n, acc):
            square = (n * n).astype(F32)
            low = yp[pl.ds(base - n, BY), :]
            high = yp[pl.ds(base + n, BY), :]
            return jnp.minimum(acc, jnp.minimum(low, high) + square)

        yo[turn] = lax.fori_loop(1, STEPS + 2, step_y, yp[pl.ds(base, BY), :], unroll=8)
        for after, tk, there in sides:
            @pl.when(there)
            def _():
                remote(
                    yo.at[turn], zb.at[2 * (1 - after), j], r3_send.at[2 * after],
                    r3_recv.at[2 * (1 - after), far_chip],
                    (i, to, tk),
                )

        if turn < NJ - 1:
            remote(yo.at[turn], zb.at[1, j], r3_send.at[1], r3_recv.at[1, far_chip], (i, to, k))
        else:
            pltpu.make_async_copy(yo.at[turn], zb.at[1, j], r3_recv.at[1, far_chip]).start()

    drain(scb, sc_recv)
    for b in range(NI):
        score_ref[:, 8 * b : 8 * b + 8, :] = scb[b]
    own_pair = jnp.where(j >= 2, 2, 0)
    pairs = tuple(enumerate((own_pair, 2 - own_pair)))

    for h, pair in pairs:
        drain(zb.at[1, pl.ds(pair, 2)], r3_recv.at[1, h])
        tz[h, 128:256, :] = zb[1, pl.ds(pair, 2)].reshape(128, BZ).T

        def near_z(n, acc):
            square = (n * n).astype(F32)
            low = tz[h, pl.ds(128 - n, 128), :]
            high = tz[h, pl.ds(128 + n, 128), :]
            return jnp.minimum(acc, jnp.minimum(low, high) + square)

        def far_z(n, halves):
            square = (n * n).astype(F32)
            low, high = halves
            low = jnp.minimum(low, tz[h, pl.ds(128 + n, 64), :] + square)
            high = jnp.minimum(high, tz[h, pl.ds(192 - n, 64), :] + square)
            return low, high

        acc = lax.fori_loop(1, 65, near_z, tz[h, 128:256, :], unroll=4)
        low, high = lax.fori_loop(65, 129, far_z, (acc[0:64], acc[64:128]), unroll=4)
        first = pair // 2
        least_ref[first, 0:64, :] = low
        least_ref[first, 64:128, :] = high

    for h, pair in pairs:
        two = pl.ds(pair, 2)
        for after, tk, there in sides:
            @pl.when(there)
            def _():
                drain(zb.at[2 * after, two], r3_recv.at[2 * after, h])

        before = zb[0, two].reshape(128, BZ).T
        tz[h, 0:128, :] = jnp.where(first_z, FAR, before)
        later = zb[2, two].reshape(128, BZ).T
        tz[h, 256:384, :] = jnp.where(last_z, FAR, later)
        first = pair // 2
        for block in range(16):
            size = 8 * block + 8

            def from_before(n, acc):
                return jnp.minimum(acc, tz[h, pl.ds(128 - n, size), :] + (n * n).astype(F32))

            def from_later(n, acc):
                return jnp.minimum(acc, tz[h, pl.ds(256 - size + n, size), :] + (n * n).astype(F32))

            span = (size - 7, size + 1)
            least_ref[first, 0:size, :] = lax.fori_loop(*span, from_before, least_ref[first, 0:size, :], unroll=8)
            rest = slice(128 - size, 128)
            least_ref[first, rest, :] = lax.fori_loop(*span, from_later, least_ref[first, rest, :], unroll=8)

    seven = pl.ds(0, NI - 1)
    drain(mr.at[seven], m_send)
    drain(r1.at[seven], r1_send)
    drain(scb.at[seven], sc_send)
    drain(rows_in.at[pl.ds(0, 2)], row_send)
    drain(yb.at[pl.ds(0, NI * NJ - 1)], r2_send)
    drain(zb.at[1, pl.ds(0, NJ - 1)], r3_send.at[1])
    for after, tk, there in sides:
        @pl.when(there)
        def _():
            drain(rims.at[after], t_send.at[after])
            drain(zb.at[2 * after], r3_send.at[2 * after])


def finish(score_in, least_ref, score_hbm, depth_hbm, depth, sems):
    copies = [pltpu.make_async_copy(score_in, score_hbm, sems.at[2])]
    copies[0].start()
    for h in range(2):
        planes = pl.ds(2 * h, 2)
        depth[planes] = (least_ref[h] * (1.0 / RADIUS)).T.reshape(2, BY, BZ)
        copies.append(pltpu.make_async_copy(depth.at[planes], depth_hbm.at[planes], sems.at[h]))
        copies[-1].start()
    for copy in copies:
        copy.wait()


def shards(features, conv_weight, mask):
    vmem = pl.BlockSpec(memory_space=pltpu.VMEM)
    hbm = pl.BlockSpec(memory_space=pltpu.HBM)
    tile = (8, BZ)
    dma = pltpu.SemaphoreType.DMA
    out = jax.ShapeDtypeStruct((BX, BY, BZ), F32)
    score, least = pl.pallas_call(
        kernel,
        out_shape=(out, jax.ShapeDtypeStruct((2, 128, BZ), F32)),
        in_specs=[hbm] * 3,
        out_specs=(vmem, vmem),
        scratch_shapes=[
            pltpu.VMEM((32, BX, BY, BZ), jnp.bfloat16),
            pltpu.VMEM((27, 32), jnp.bfloat16),
            pltpu.VMEM((BX, BY, BZ), jnp.int32),
            pltpu.VMEM((288, 512), jnp.bfloat16),
            pltpu.VMEM((3, PLANES, BY + 16, BZ), F32),
            pltpu.VMEM((PLANES, BY + 16, BZ), F32),
            pltpu.VMEM((5, *tile), F32),
            pltpu.VMEM(tile, F32),
            pltpu.VMEM((NI, PLANES, *tile), F32),
            pltpu.VMEM((2, *tile), F32),
            pltpu.VMEM((NI, *tile), F32),
            pltpu.VMEM((NI, BX, *tile), jnp.int32),
            pltpu.VMEM((32, *tile), F32),
            pltpu.VMEM((NI, BX, *tile), F32),
            pltpu.VMEM((32, *tile), F32),
            pltpu.VMEM((32, *tile), F32),
            pltpu.VMEM((32, *tile), F32),
            pltpu.VMEM((512, BZ), F32),
            pltpu.VMEM((NJ, BY, BZ), F32),
            pltpu.VMEM((3, NJ, BY, BZ), F32),
            pltpu.VMEM((2, 384, BZ), F32),
            dma((3,)),
        ] + [dma] * 10 + [dma((2,))] * 2 + [dma((3,)), dma((3, 2))],
        compiler_params=pltpu.CompilerParams(
            collective_id=0, has_side_effects=True, vmem_limit_bytes=40 * 1024 * 1024
        ),
    )(*[pltpu.with_memory_space_constraint(x, pltpu.HBM) for x in (features, conv_weight, mask)])
    return pl.pallas_call(
        finish,
        out_shape=(out, out),
        in_specs=[vmem] * 2,
        out_specs=(hbm, hbm),
        scratch_shapes=[pltpu.VMEM((BX, BY, BZ), F32), dma((3,))],
        compiler_params=pltpu.CompilerParams(vmem_limit_bytes=2 * 1024 * 1024),
    )(score, least)


def solution(mesh):
    in_specs = (P(None, "gx", "gy", "gz"), P(), P("gx", "gy", "gz"))
    out_specs = (P("gx", "gy", "gz"), P("gx", "gy", "gz"))
    return jax.shard_map(shards, mesh=mesh, in_specs=in_specs, out_specs=out_specs, check_vma=False)
```

```python
import functools

import jax
import jax.numpy as jnp
from jax import lax
from jax.experimental import pallas as pl
from jax.experimental.pallas import tpu as pltpu
from jax.sharding import PartitionSpec as P

MESH = pl.DeviceIdType.MESH
RADIUS = 128
CEILING = float(RADIUS * RADIUS)
FAR = 1.0e9
F32 = jnp.float32
BX, BY, BZ = 4, 64, 128
NI, NJ, NK = 8, 4, 8
PLANES = BX + 2
STEPS = RADIUS - 1


def iota(shape, axis):
    return lax.broadcasted_iota(jnp.int32, shape, axis)


def banded_weights(w_ref, wb_ref):
    rows, cols = 9 * 32, 32 * 16
    weights = w_ref[...]
    row = iota((rows, 27), 0)
    tap = iota((rows, 27), 1)
    group = row // 32
    spread = (iota((32, cols), 1) // 16 == iota((32, cols), 0)).astype(jnp.bfloat16)
    gap = iota((rows, cols), 1) % 16 - (iota((rows, cols), 0) % 32 - 8)
    total = jnp.zeros((rows, cols), F32)
    for b in range(3):
        pick = (tap == (group // 3) * 9 + 3 * b + group % 3).astype(jnp.bfloat16)
        own = jnp.dot(pick, weights, preferred_element_type=F32).astype(jnp.bfloat16)
        wide = jnp.dot(own, spread, preferred_element_type=F32)
        total = jnp.where(gap == b - 1, wide, total)
    wb_ref[...] = total.astype(jnp.bfloat16)


def kernel(
    f_hbm, w_hbm, m_hbm, score_ref, least_ref,
    f_ref, w_ref, m_ref, wb, s3, s, pack, rim, r1, rims, rims_y, rows_in, mb, mr, sc, scb, xin, xo, yb, yp, yo, zb, tz,
    in_sems, m_send, m_recv, r1_send, r1_recv, row_send, row_recv, sc_send, sc_recv,
    r2_send, r2_recv, t_send, t_recv, ry_send, ry_recv, r3_send, r3_recv,
):
    i, j, k = lax.axis_index("gx"), lax.axis_index("gy"), lax.axis_index("gz")
    loads = [
        pltpu.make_async_copy(source, target, in_sems.at[n])
        for n, (source, target) in enumerate(((w_hbm, w_ref), (f_hbm, f_ref), (m_hbm, m_ref)))
    ]
    for load in loads:
        load.start()

    def around(position, size):
        return [position] + [
            jnp.where(position >= size - d, position - (size - d), position + d) for d in range(1, size)
        ]

    xs_of, ys_of = around(i, NI), around(j, NJ)
    xs_of = [xs_of[d] for d in (0, 3, 5, 4, 1, 7, 2, 6)]
    ys_far = [ys_of[d] for d in (2, 3, 1, 0)]
    first_z, last_z = k == 0, k == NK - 1
    sides = ((1, k + 1, jnp.logical_not(last_z)), (0, k - 1, jnp.logical_not(first_z)))
    side_count = 2 - first_z.astype(jnp.int32) - last_z.astype(jnp.int32)

    barrier = pltpu.get_barrier_semaphore()

    def greet(*device):
        pl.semaphore_signal(barrier, inc=1, device_id=device, device_id_type=MESH)

    for _, tk, there in sides:
        @pl.when(there)
        def _():
            for ti in xs_of:
                greet(ti, j, tk)

    for ti in xs_of[1:] + [i]:
        for tj in ys_far:
            if ti is not i or tj is not j:
                greet(ti, tj, k)
    at_end = (i == 0) | (i == NI - 1)
    end_j = jnp.where(i == 0, ys_of[NJ - 1], ys_of[1])
    for _, tk, there in sides:
        @pl.when(there & at_end)
        def _():
            for ti in range(NI):
                greet(ti, end_j, tk)

    greeted = NI * NJ - 1 + side_count * (NI + 2)

    loads[0].wait()
    banded_weights(w_ref, wb)
    s3[...] = jnp.zeros_like(s3)
    loads[1].wait()

    def conv_block(q, carry):
        start = pl.multiple_of(q * 16, 16)
        for xs in range(BX):
            block = f_ref[:, xs, pl.ds(start, 16), :].reshape(32 * 16, BZ)
            part = jnp.dot(wb[...], block, preferred_element_type=F32)
            for a in range(3):
                for c in range(3):
                    at = (3 * a + c) * 32
                    s3[c, xs - a + 2, pl.ds(start, 32), :] += part[at : at + 32]
        return carry

    lax.fori_loop(0, BY // 16, conv_block, 0)

    lane = iota((8, BZ), 1)
    sub = iota((8, BZ), 0)
    edge = (lane == 0) | (lane == BZ - 1)
    zero = jnp.zeros((8, BZ), F32)
    pack[...] = jnp.zeros_like(pack)

    def shift_plane(p, tile):
        for t in range(10):
            rows = pl.ds(8 * t, 8)
            right = pltpu.roll(s3[0, p, rows, :], 1, 1)
            left = pltpu.roll(s3[2, p, rows, :], BZ - 1, 1)
            mine = s3[1, p, rows, :] + jnp.where(lane == 0, 0.0, right) + jnp.where(lane == BZ - 1, 0.0, left)
            s[p, rows, :] = mine
            outer = jnp.where(lane == 0, right, left)
            if t == 0:
                pack[1, pl.ds(p, 1), :] = mine[7:8]
                pack[2, pl.ds(p, 1), :] = outer[7:8]
            elif t == 9:
                pack[3, pl.ds(p, 1), :] = mine[0:1]
                pack[4, pl.ds(p, 1), :] = outer[0:1]
            else:
                v = 2 * (p * 8 + t - 1)
                moved = pltpu.roll(outer, v, 1)
                tile = jnp.where((lane == v) | (lane == (v + BZ - 1) % BZ), moved, tile)
        return tile

    tile = lax.fori_loop(0, PLANES, shift_plane, zero)
    for near, v in ((2, 96), (4, 98)):
        tile = jnp.where((lane == v) | (lane == v - 1), pltpu.roll(pack[near], v, 1), tile)
    rim[...] = tile
    far = jnp.full((128, BZ), FAR, F32)
    yp[0:128] = far
    yp[384:512] = far
    for h in range(2):
        tz[h, 0:128] = far
        tz[h, 256:384] = far

    @pl.when(jnp.logical_not(at_end))
    def _():
        rows_in[...] = jnp.zeros_like(rows_in)
        rims_y[...] = jnp.zeros_like(rims_y)

    loads[2].wait()
    for b in range(NI):
        mb[b] = m_ref[:, 8 * b : 8 * b + 8, :].reshape(32, BZ).astype(F32).astype(jnp.bfloat16)
    pl.semaphore_wait(barrier, greeted)

    def remote(source, target, send, recv, device):
        pltpu.make_async_remote_copy(
            source, target, send, recv, device_id=device, device_id_type=MESH
        ).start()

    def drain(ref, semaphore):
        pltpu.make_async_copy(ref, ref, semaphore).wait()

    ends = ((NI - 1, ys_of[NJ - 1], 1), (0, ys_of[1], 3))
    for after, tk, there in sides:
        @pl.when(there)
        def _():
            for ti in xs_of[1:] + [i]:
                remote(rim, rims.at[1 - after, i], t_send.at[after], t_recv.at[1 - after], (ti, j, tk))
            for ti, tj, near in ends:
                remote(
                    rim, rims_y.at[1 - after, i], ry_send.at[after], ry_recv.at[1 - after], (ti, tj, tk)
                )

    def part_rows(to):
        return s.at[:, pl.ds(pl.multiple_of(8 + to * 8, 8), 8), :]

    for ti in xs_of[1:]:
        remote(part_rows(ti), r1.at[i], r1_send, r1_recv, (ti, j, k))
    for ti, tj, near in ends:
        remote(pack.at[near], rows_in.at[i], row_send, row_recv, (ti, tj, k))
    pltpu.make_async_copy(part_rows(i), r1.at[i], r1_recv).start()
    def mask_rows(to):
        return mb.at[to]

    for ti in xs_of[1:]:
        remote(mask_rows(ti), mr.at[i], m_send, m_recv, (ti, j, k))
    pltpu.make_async_copy(mask_rows(i), mr.at[i], m_recv).start()

    outside = ((i == 0) & (j == 0)) | ((i == NI - 1) & (j == NJ - 1))

    @pl.when(at_end)
    def _():
        drain(rows_in, row_recv)

    for after, tk, there in sides:
        @pl.when(there & at_end)
        def _():
            drain(rims_y.at[after], ry_recv.at[after])

        @pl.when(there)
        def _():
            drain(rims.at[after], t_recv.at[after])

    drain(r1, r1_recv)
    drain(mr, m_recv)

    end_row = sub == jnp.where(i == 0, 0, 7)
    parts = []
    for b in range(NI):
        both = jnp.where(
            lane % 2 == 0, jnp.where(first_z, zero, rims[0, b]), jnp.where(last_z, zero, rims[1, b])
        )
        both = pltpu.roll(both, BZ - 2 * i, 1)
        corner = jnp.where(
            lane % 2 == 0, jnp.where(first_z, zero, rims_y[0, b]), jnp.where(last_z, zero, rims_y[1, b])
        )
        corner = pltpu.roll(corner, jnp.where(i == 0, BZ - 98, BZ - 96), 1)
        rows = rows_in[b] + jnp.where(edge, corner, 0.0)
        rows = jnp.where(outside, zero, rows)
        planes = []
        for p in range(PLANES):
            moved = both if p == 0 else pltpu.roll(both, BZ - 16 * p, 1)
            planes.append(
                r1[b, p]
                + jnp.where(edge, moved, 0.0)
                + jnp.where(end_row, jnp.broadcast_to(rows[p : p + 1], (8, BZ)), 0.0)
            )
        parts.append(planes)
    for b in range(NI):
        inside = mr[b].astype(F32)
        for a in range(BX):
            value = parts[b][a + 1]
            if a == 0 and b > 0:
                value += parts[b - 1][BX + 1]
            if a == BX - 1 and b < NI - 1:
                value += parts[b + 1][0]
            x = BX * b + a
            sc[x] = value
            cost = CEILING / (1.0 + jnp.exp(-value))
            xin[x] = jnp.where(inside[8 * a : 8 * a + 8] > 0.5, CEILING, cost)

    acc = xin[...]
    for n in range(1, 32):
        square = float(n * n)
        if n < 16:
            pair = jnp.minimum(xin[0 : 32 - 2 * n], xin[2 * n : 32]) + square
            least = jnp.concatenate([xin[n : 2 * n] + square, pair, xin[32 - 2 * n : 32 - n] + square], axis=0)
            acc = jnp.minimum(acc, least)
        else:
            low = jnp.minimum(acc[0 : 32 - n], xin[n:32] + square)
            high = jnp.minimum(acc[n:32], xin[0 : 32 - n] + square)
            middle = [acc[32 - n : n]] if n > 16 else []
            acc = jnp.concatenate([low, *middle, high], axis=0)
    xo[...] = acc

    for ti in xs_of[1:] + [i]:
        for tj in ys_far:
            if ti is not i or tj is not j:
                remote(xo.at[ti * NJ + tj], yb.at[j * NI + i], r2_send, r2_recv, (ti, tj, k))
    pltpu.make_async_copy(xo.at[i * NJ + j], yb.at[j * NI + i], r2_recv).start()

    for ti in xs_of[1:]:
        remote(sc.at[pl.ds(ti * BX, BX)], scb.at[i], sc_send, sc_recv, (ti, j, k))
    pltpu.make_async_copy(sc.at[pl.ds(i * BX, BX)], scb.at[i], sc_recv).start()

    drain(yb, r2_recv)
    yp[128:384] = yb[...].reshape(256, BZ)

    for turn, to in enumerate((ys_of[2], NJ - 1 - j, NJ - 1 - ys_of[2], j)):
        base = pl.multiple_of(128 + to * BY, BY)
        far_chip = 1 if turn < 2 else 0

        def step_y(n, acc):
            square = (n * n).astype(F32)
            low = yp[pl.ds(base - n, BY), :]
            high = yp[pl.ds(base + n, BY), :]
            return jnp.minimum(acc, jnp.minimum(low, high) + square)

        yo[turn] = lax.fori_loop(1, STEPS + 2, step_y, yp[pl.ds(base, BY), :], unroll=8)
        for after, tk, there in sides:
            @pl.when(there)
            def _():
                remote(
                    yo.at[turn], zb.at[2 * (1 - after), j], r3_send.at[2 * after],
                    r3_recv.at[2 * (1 - after), far_chip],
                    (i, to, tk),
                )

        if turn < NJ - 1:
            remote(yo.at[turn], zb.at[1, j], r3_send.at[1], r3_recv.at[1, far_chip], (i, to, k))
        else:
            pltpu.make_async_copy(yo.at[turn], zb.at[1, j], r3_recv.at[1, far_chip]).start()

    drain(scb, sc_recv)
    for b in range(NI):
        score_ref[:, 8 * b : 8 * b + 8, :] = scb[b]
    own_pair = jnp.where(j >= 2, 2, 0)
    pairs = tuple(enumerate((own_pair, 2 - own_pair)))

    for h, pair in pairs:
        drain(zb.at[1, pl.ds(pair, 2)], r3_recv.at[1, h])
        tz[h, 128:256, :] = zb[1, pl.ds(pair, 2)].reshape(128, BZ).T

        def near_z(n, acc):
            square = (n * n).astype(F32)
            low = tz[h, pl.ds(128 - n, 128), :]
            high = tz[h, pl.ds(128 + n, 128), :]
            return jnp.minimum(acc, jnp.minimum(low, high) + square)

        def far_z(n, halves):
            square = (n * n).astype(F32)
            low, high = halves
            low = jnp.minimum(low, tz[h, pl.ds(128 + n, 64), :] + square)
            high = jnp.minimum(high, tz[h, pl.ds(192 - n, 64), :] + square)
            return low, high

        acc = lax.fori_loop(1, 65, near_z, tz[h, 128:256, :], unroll=4)
        low, high = lax.fori_loop(65, 129, far_z, (acc[0:64], acc[64:128]), unroll=4)
        first = pair // 2
        least_ref[first, 0:64, :] = low
        least_ref[first, 64:128, :] = high

    for h, pair in pairs:
        two = pl.ds(pair, 2)
        for after, tk, there in sides:
            @pl.when(there)
            def _():
                drain(zb.at[2 * after, two], r3_recv.at[2 * after, h])

        before = zb[0, two].reshape(128, BZ).T
        tz[h, 0:128, :] = jnp.where(first_z, FAR, before)
        later = zb[2, two].reshape(128, BZ).T
        tz[h, 256:384, :] = jnp.where(last_z, FAR, later)
        first = pair // 2
        for block in range(16):
            size = 8 * block + 8

            def from_before(n, acc):
                return jnp.minimum(acc, tz[h, pl.ds(128 - n, size), :] + (n * n).astype(F32))

            def from_later(n, acc):
                return jnp.minimum(acc, tz[h, pl.ds(256 - size + n, size), :] + (n * n).astype(F32))

            span = (size - 7, size + 1)
            least_ref[first, 0:size, :] = lax.fori_loop(*span, from_before, least_ref[first, 0:size, :], unroll=8)
            rest = slice(128 - size, 128)
            least_ref[first, rest, :] = lax.fori_loop(*span, from_later, least_ref[first, rest, :], unroll=8)

    seven = pl.ds(0, NI - 1)
    drain(mr.at[seven], m_send)
    drain(r1.at[seven], r1_send)
    drain(scb.at[seven], sc_send)
    drain(rows_in.at[pl.ds(0, 2)], row_send)
    drain(yb.at[pl.ds(0, NI * NJ - 1)], r2_send)
    drain(zb.at[1, pl.ds(0, NJ - 1)], r3_send.at[1])
    for after, tk, there in sides:
        @pl.when(there)
        def _():
            drain(rims_y.at[after, pl.ds(0, 2)], ry_send.at[after])
            drain(rims.at[after], t_send.at[after])
            drain(zb.at[2 * after], r3_send.at[2 * after])


def finish(score_in, least_ref, score_hbm, depth_hbm, depth, sems):
    copies = [pltpu.make_async_copy(score_in, score_hbm, sems.at[2])]
    copies[0].start()
    for h in range(2):
        planes = pl.ds(2 * h, 2)
        depth[planes] = (least_ref[h] * (1.0 / RADIUS)).T.reshape(2, BY, BZ)
        copies.append(pltpu.make_async_copy(depth.at[planes], depth_hbm.at[planes], sems.at[h]))
        copies[-1].start()
    for copy in copies:
        copy.wait()


def shards(features, conv_weight, mask):
    vmem = pl.BlockSpec(memory_space=pltpu.VMEM)
    hbm = pl.BlockSpec(memory_space=pltpu.HBM)
    tile = (8, BZ)
    dma = pltpu.SemaphoreType.DMA
    out = jax.ShapeDtypeStruct((BX, BY, BZ), F32)
    score, least = pl.pallas_call(
        kernel,
        out_shape=(out, jax.ShapeDtypeStruct((2, 128, BZ), F32)),
        in_specs=[hbm] * 3,
        out_specs=(vmem, vmem),
        scratch_shapes=[
            pltpu.VMEM((32, BX, BY, BZ), jnp.bfloat16),
            pltpu.VMEM((27, 32), jnp.bfloat16),
            pltpu.VMEM((BX, BY, BZ), jnp.int32),
            pltpu.VMEM((288, 512), jnp.bfloat16),
            pltpu.VMEM((3, PLANES, BY + 16, BZ), F32),
            pltpu.VMEM((PLANES, BY + 16, BZ), F32),
            pltpu.VMEM((5, *tile), F32),
            pltpu.VMEM(tile, F32),
            pltpu.VMEM((NI, PLANES, *tile), F32),
            pltpu.VMEM((2, NI, *tile), F32),
            pltpu.VMEM((2, NI, *tile), F32),
            pltpu.VMEM((NI, *tile), F32),
            pltpu.VMEM((NI, 32, BZ), jnp.bfloat16),
            pltpu.VMEM((NI, 32, BZ), jnp.bfloat16),
            pltpu.VMEM((32, *tile), F32),
            pltpu.VMEM((NI, BX, *tile), F32),
            pltpu.VMEM((32, *tile), F32),
            pltpu.VMEM((32, *tile), F32),
            pltpu.VMEM((32, *tile), F32),
            pltpu.VMEM((512, BZ), F32),
            pltpu.VMEM((NJ, BY, BZ), F32),
            pltpu.VMEM((3, NJ, BY, BZ), F32),
            pltpu.VMEM((2, 384, BZ), F32),
            dma((3,)),
        ] + [dma] * 10 + [dma((2,))] * 4 + [dma((3,)), dma((3, 2))],
        compiler_params=pltpu.CompilerParams(
            collective_id=0, has_side_effects=True, vmem_limit_bytes=40 * 1024 * 1024
        ),
    )(*[pltpu.with_memory_space_constraint(x, pltpu.HBM) for x in (features, conv_weight, mask)])
    return pl.pallas_call(
        finish,
        out_shape=(out, out),
        in_specs=[vmem] * 2,
        out_specs=(hbm, hbm),
        scratch_shapes=[pltpu.VMEM((BX, BY, BZ), F32), dma((3,))],
        compiler_params=pltpu.CompilerParams(vmem_limit_bytes=2 * 1024 * 1024),
    )(score, least)


def solution(mesh):
    in_specs = (P(None, "gx", "gy", "gz"), P(), P("gx", "gy", "gz"))
    out_specs = (P("gx", "gy", "gz"), P("gx", "gy", "gz"))
    return jax.shard_map(shards, mesh=mesh, in_specs=in_specs, out_specs=out_specs, check_vma=False)
```

```python
import functools

import jax
import jax.numpy as jnp
from jax import lax
from jax.experimental import pallas as pl
from jax.experimental.pallas import tpu as pltpu
from jax.sharding import PartitionSpec as P

MESH = pl.DeviceIdType.MESH
RADIUS = 128
CEILING = float(RADIUS * RADIUS)
FAR = 1.0e9
F32 = jnp.float32
BX, BY, BZ = 4, 64, 128
NI, NJ, NK = 8, 4, 8
PLANES = BX + 2
STEPS = RADIUS - 1


def iota(shape, axis):
    return lax.broadcasted_iota(jnp.int32, shape, axis)


def banded_weights(w_ref, wb_ref):
    rows, cols = 9 * 32, 32 * 16
    weights = w_ref[...]
    row = iota((rows, 27), 0)
    tap = iota((rows, 27), 1)
    group = row // 32
    spread = (iota((32, cols), 1) // 16 == iota((32, cols), 0)).astype(jnp.bfloat16)
    gap = iota((rows, cols), 1) % 16 - (iota((rows, cols), 0) % 32 - 8)
    total = jnp.zeros((rows, cols), F32)
    for b in range(3):
        pick = (tap == (group // 3) * 9 + 3 * b + group % 3).astype(jnp.bfloat16)
        own = jnp.dot(pick, weights, preferred_element_type=F32).astype(jnp.bfloat16)
        wide = jnp.dot(own, spread, preferred_element_type=F32)
        total = jnp.where(gap == b - 1, wide, total)
    wb_ref[...] = total.astype(jnp.bfloat16)


def kernel(
    f_hbm, w_hbm, m_hbm, score_ref, least_ref,
    f_ref, w_ref, m_ref, wb, s3, s, pack, rim, r1, rims, rims_y, rows_in, mb, mr, sc, scb, xin, xo, yb, yp, yo, zb, tz,
    in_sems, m_send, m_recv, r1_send, r1_recv, row_send, row_recv, sc_send, sc_recv,
    r2_send, r2_recv, t_send, t_recv, ry_send, ry_recv, r3_send, r3_recv,
):
    i, j, k = lax.axis_index("gx"), lax.axis_index("gy"), lax.axis_index("gz")
    loads = [
        pltpu.make_async_copy(source, target, in_sems.at[n])
        for n, (source, target) in enumerate(((w_hbm, w_ref), (f_hbm, f_ref), (m_hbm, m_ref)))
    ]
    for load in loads:
        load.start()

    def around(position, size):
        return [position] + [
            jnp.where(position >= size - d, position - (size - d), position + d) for d in range(1, size)
        ]

    xs_of, ys_of = around(i, NI), around(j, NJ)
    xs_of = [xs_of[d] for d in (0, 3, 5, 4, 1, 7, 2, 6)]
    ys_far = [ys_of[d] for d in (2, 3, 1, 0)]
    first_z, last_z = k == 0, k == NK - 1
    sides = ((1, k + 1, jnp.logical_not(last_z)), (0, k - 1, jnp.logical_not(first_z)))
    side_count = 2 - first_z.astype(jnp.int32) - last_z.astype(jnp.int32)

    barrier = pltpu.get_barrier_semaphore()

    def greet(*device):
        pl.semaphore_signal(barrier, inc=1, device_id=device, device_id_type=MESH)

    for _, tk, there in sides:
        @pl.when(there)
        def _():
            for ti in xs_of:
                greet(ti, j, tk)

    for ti in xs_of[1:] + [i]:
        for tj in ys_far:
            if ti is not i or tj is not j:
                greet(ti, tj, k)
    at_end = (i == 0) | (i == NI - 1)
    end_j = jnp.where(i == 0, ys_of[NJ - 1], ys_of[1])
    for _, tk, there in sides:
        @pl.when(there & at_end)
        def _():
            for ti in range(NI):
                greet(ti, end_j, tk)

    greeted = NI * NJ - 1 + side_count * (NI + 2)

    loads[0].wait()
    banded_weights(w_ref, wb)
    s3[...] = jnp.zeros_like(s3)
    loads[1].wait()

    def conv_block(q, carry):
        start = pl.multiple_of(q * 16, 16)
        for xs in range(BX):
            block = f_ref[:, xs, pl.ds(start, 16), :].reshape(32 * 16, BZ)
            part = jnp.dot(wb[...], block, preferred_element_type=F32)
            for a in range(3):
                for c in range(3):
                    at = (3 * a + c) * 32
                    s3[c, xs - a + 2, pl.ds(start, 32), :] += part[at : at + 32]
        return carry

    lax.fori_loop(0, BY // 16, conv_block, 0)

    lane = iota((8, BZ), 1)
    sub = iota((8, BZ), 0)
    edge = (lane == 0) | (lane == BZ - 1)
    zero = jnp.zeros((8, BZ), F32)
    pack[...] = jnp.zeros_like(pack)

    def shift_plane(p, tile):
        for t in range(10):
            rows = pl.ds(8 * t, 8)
            right = pltpu.roll(s3[0, p, rows, :], 1, 1)
            left = pltpu.roll(s3[2, p, rows, :], BZ - 1, 1)
            mine = s3[1, p, rows, :] + jnp.where(lane == 0, 0.0, right) + jnp.where(lane == BZ - 1, 0.0, left)
            s[p, rows, :] = mine
            outer = jnp.where(lane == 0, right, left)
            if t == 0:
                pack[1, pl.ds(p, 1), :] = mine[7:8]
                pack[2, pl.ds(p, 1), :] = outer[7:8]
            elif t == 9:
                pack[3, pl.ds(p, 1), :] = mine[0:1]
                pack[4, pl.ds(p, 1), :] = outer[0:1]
            else:
                v = 2 * (p * 8 + t - 1)
                moved = pltpu.roll(outer, v, 1)
                tile = jnp.where((lane == v) | (lane == (v + BZ - 1) % BZ), moved, tile)
        return tile

    tile = lax.fori_loop(0, PLANES, shift_plane, zero)
    for near, v in ((2, 96), (4, 98)):
        tile = jnp.where((lane == v) | (lane == v - 1), pltpu.roll(pack[near], v, 1), tile)
    rim[...] = tile
    far = jnp.full((128, BZ), FAR, F32)
    yp[0:128] = far
    yp[384:512] = far
    for h in range(2):
        tz[h, 0:128] = far
        tz[h, 256:384] = far

    @pl.when(jnp.logical_not(at_end))
    def _():
        rows_in[...] = jnp.zeros_like(rows_in)
        rims_y[...] = jnp.zeros_like(rims_y)

    loads[2].wait()
    for b in range(NI):
        mb[b] = m_ref[:, 8 * b : 8 * b + 8, :].reshape(32, BZ).astype(F32).astype(jnp.bfloat16)
    pl.semaphore_wait(barrier, greeted)

    def remote(source, target, send, recv, device):
        pltpu.make_async_remote_copy(
            source, target, send, recv, device_id=device, device_id_type=MESH
        ).start()

    def drain(ref, semaphore):
        pltpu.make_async_copy(ref, ref, semaphore).wait()

    ends = ((NI - 1, ys_of[NJ - 1], 1), (0, ys_of[1], 3))
    for after, tk, there in sides:
        @pl.when(there)
        def _():
            for ti in xs_of[1:] + [i]:
                remote(rim, rims.at[1 - after, i], t_send.at[after], t_recv.at[1 - after], (ti, j, tk))
            for ti, tj, near in ends:
                remote(
                    rim, rims_y.at[1 - after, i], ry_send.at[after], ry_recv.at[1 - after], (ti, tj, tk)
                )

    def part_rows(to):
        return s.at[:, pl.ds(pl.multiple_of(8 + to * 8, 8), 8), :]

    for ti in xs_of[1:]:
        remote(part_rows(ti), r1.at[i], r1_send, r1_recv, (ti, j, k))
    for ti, tj, near in ends:
        remote(pack.at[near], rows_in.at[i], row_send, row_recv, (ti, tj, k))
    pltpu.make_async_copy(part_rows(i), r1.at[i], r1_recv).start()
    def mask_rows(to):
        return mb.at[to]

    for ti in xs_of[1:]:
        remote(mask_rows(ti), mr.at[i], m_send, m_recv, (ti, j, k))
    pltpu.make_async_copy(mask_rows(i), mr.at[i], m_recv).start()

    outside = ((i == 0) & (j == 0)) | ((i == NI - 1) & (j == NJ - 1))

    @pl.when(at_end)
    def _():
        drain(rows_in, row_recv)

    for after, tk, there in sides:
        @pl.when(there & at_end)
        def _():
            drain(rims_y.at[after], ry_recv.at[after])

        @pl.when(there)
        def _():
            drain(rims.at[after], t_recv.at[after])

    drain(r1, r1_recv)
    drain(mr, m_recv)

    end_row = sub == jnp.where(i == 0, 0, 7)
    parts = []
    for b in range(NI):
        both = jnp.where(
            lane % 2 == 0, jnp.where(first_z, zero, rims[0, b]), jnp.where(last_z, zero, rims[1, b])
        )
        both = pltpu.roll(both, BZ - 2 * i, 1)
        corner = jnp.where(
            lane % 2 == 0, jnp.where(first_z, zero, rims_y[0, b]), jnp.where(last_z, zero, rims_y[1, b])
        )
        corner = pltpu.roll(corner, jnp.where(i == 0, BZ - 98, BZ - 96), 1)
        rows = rows_in[b] + jnp.where(edge, corner, 0.0)
        rows = jnp.where(outside, zero, rows)
        planes = []
        for p in range(PLANES):
            moved = both if p == 0 else pltpu.roll(both, BZ - 16 * p, 1)
            planes.append(
                r1[b, p]
                + jnp.where(edge, moved, 0.0)
                + jnp.where(end_row, jnp.broadcast_to(rows[p : p + 1], (8, BZ)), 0.0)
            )
        parts.append(planes)
    for b in range(NI):
        inside = mr[b].astype(F32)
        for a in range(BX):
            value = parts[b][a + 1]
            if a == 0 and b > 0:
                value += parts[b - 1][BX + 1]
            if a == BX - 1 and b < NI - 1:
                value += parts[b + 1][0]
            x = BX * b + a
            sc[x] = value
            cost = CEILING / (1.0 + jnp.exp(-value))
            xin[x] = jnp.where(inside[8 * a : 8 * a + 8] > 0.5, CEILING, cost)

    acc = xin[...]
    for n in range(1, 32):
        square = float(n * n)
        if n < 16:
            pair = jnp.minimum(xin[0 : 32 - 2 * n], xin[2 * n : 32]) + square
            least = jnp.concatenate([xin[n : 2 * n] + square, pair, xin[32 - 2 * n : 32 - n] + square], axis=0)
            acc = jnp.minimum(acc, least)
        else:
            low = jnp.minimum(acc[0 : 32 - n], xin[n:32] + square)
            high = jnp.minimum(acc[n:32], xin[0 : 32 - n] + square)
            middle = [acc[32 - n : n]] if n > 16 else []
            acc = jnp.concatenate([low, *middle, high], axis=0)
    xo[...] = acc

    for ti in xs_of[1:] + [i]:
        for tj in ys_far:
            if ti is not i or tj is not j:
                remote(xo.at[ti * NJ + tj], yb.at[j * NI + i], r2_send, r2_recv, (ti, tj, k))
    pltpu.make_async_copy(xo.at[i * NJ + j], yb.at[j * NI + i], r2_recv).start()

    for ti in xs_of[1:]:
        remote(sc.at[pl.ds(ti * BX, BX)], scb.at[i], sc_send, sc_recv, (ti, j, k))
    pltpu.make_async_copy(sc.at[pl.ds(i * BX, BX)], scb.at[i], sc_recv).start()

    drain(yb, r2_recv)
    yp[128:384] = yb[...].reshape(256, BZ)

    for turn, to in enumerate((ys_of[2], NJ - 1 - j, NJ - 1 - ys_of[2], j)):
        base = pl.multiple_of(128 + to * BY, BY)
        far_chip = 1 if turn < 2 else 0

        def step_y(n, acc):
            square = (n * n).astype(F32)
            low = yp[pl.ds(base - n, BY), :]
            high = yp[pl.ds(base + n, BY), :]
            return jnp.minimum(acc, jnp.minimum(low, high) + square)

        yo[turn] = lax.fori_loop(1, STEPS + 2, step_y, yp[pl.ds(base, BY), :], unroll=8)
        for after, tk, there in sides:
            @pl.when(there)
            def _():
                remote(
                    yo.at[turn], zb.at[2 * (1 - after), j], r3_send.at[2 * after],
                    r3_recv.at[2 * (1 - after), far_chip],
                    (i, to, tk),
                )

        if turn < NJ - 1:
            remote(yo.at[turn], zb.at[1, j], r3_send.at[1], r3_recv.at[1, far_chip], (i, to, k))
        else:
            pltpu.make_async_copy(yo.at[turn], zb.at[1, j], r3_recv.at[1, far_chip]).start()

    drain(scb, sc_recv)
    for b in range(NI):
        score_ref[:, 8 * b : 8 * b + 8, :] = scb[b]
    own_pair = jnp.where(j >= 2, 2, 0)
    pairs = tuple(enumerate((own_pair, 2 - own_pair)))

    for h, pair in pairs:
        drain(zb.at[1, pl.ds(pair, 2)], r3_recv.at[1, h])
        tz[h, 128:256, :] = zb[1, pl.ds(pair, 2)].reshape(128, BZ).T

        def near_z(n, acc):
            square = (n * n).astype(F32)
            low = tz[h, pl.ds(128 - n, 128), :]
            high = tz[h, pl.ds(128 + n, 128), :]
            return jnp.minimum(acc, jnp.minimum(low, high) + square)

        def far_z(n, halves):
            square = (n * n).astype(F32)
            low, high = halves
            low = jnp.minimum(low, tz[h, pl.ds(128 + n, 64), :] + square)
            high = jnp.minimum(high, tz[h, pl.ds(192 - n, 64), :] + square)
            return low, high

        acc = lax.fori_loop(1, 65, near_z, tz[h, 128:256, :], unroll=4)
        low, high = lax.fori_loop(65, 129, far_z, (acc[0:64], acc[64:128]), unroll=4)
        first = pair // 2
        least_ref[first, 0:64, :] = low
        least_ref[first, 64:128, :] = high

    for h, pair in pairs:
        two = pl.ds(pair, 2)
        for after, tk, there in sides:
            @pl.when(there)
            def _():
                drain(zb.at[2 * after, two], r3_recv.at[2 * after, h])

        before = zb[0, two].reshape(128, BZ).T
        tz[h, 0:128, :] = jnp.where(first_z, FAR, before)
        later = zb[2, two].reshape(128, BZ).T
        tz[h, 256:384, :] = jnp.where(last_z, FAR, later)
        first = pair // 2
        for block in range(8):
            size = 8 * block + 8

            def from_before(n, acc):
                return jnp.minimum(acc, tz[h, pl.ds(128 - n, size), :] + (n * n).astype(F32))

            def from_later(n, acc):
                return jnp.minimum(acc, tz[h, pl.ds(256 - size + n, size), :] + (n * n).astype(F32))

            span = (size - 7, size + 1)
            least_ref[first, 0:size, :] = lax.fori_loop(*span, from_before, least_ref[first, 0:size, :], unroll=8)
            rest = slice(128 - size, 128)
            least_ref[first, rest, :] = lax.fori_loop(*span, from_later, least_ref[first, rest, :], unroll=8)

        for block in range(8, 16):
            size = 8 * block + 8
            rest = 128 - size

            def from_both(n, parts):
                square = (n * n).astype(F32)
                middle = jnp.minimum(
                    tz[h, pl.ds(128 + rest - n, size - rest), :], tz[h, pl.ds(128 + rest + n, size - rest), :]
                )
                found = [jnp.minimum(parts[0], middle + square)]
                if rest:
                    found.append(jnp.minimum(parts[1], tz[h, pl.ds(128 - n, rest), :] + square))
                    found.append(jnp.minimum(parts[2], tz[h, pl.ds(128 + size + n, rest), :] + square))
                return tuple(found)

            places = [slice(rest, size)] + ([slice(0, rest), slice(size, 128)] if rest else [])
            found = lax.fori_loop(
                size - 7, size + 1, from_both, tuple(least_ref[first, place, :] for place in places), unroll=8
            )
            for place, value in zip(places, found):
                least_ref[first, place, :] = value

    seven = pl.ds(0, NI - 1)
    drain(mr.at[seven], m_send)
    drain(r1.at[seven], r1_send)
    drain(scb.at[seven], sc_send)
    drain(rows_in.at[pl.ds(0, 2)], row_send)
    drain(yb.at[pl.ds(0, NI * NJ - 1)], r2_send)
    drain(zb.at[1, pl.ds(0, NJ - 1)], r3_send.at[1])
    for after, tk, there in sides:
        @pl.when(there)
        def _():
            drain(rims_y.at[after, pl.ds(0, 2)], ry_send.at[after])
            drain(rims.at[after], t_send.at[after])
            drain(zb.at[2 * after], r3_send.at[2 * after])


def finish(score_in, least_ref, score_hbm, depth_hbm, depth, sems):
    copies = [pltpu.make_async_copy(score_in, score_hbm, sems.at[2])]
    copies[0].start()
    for h in range(2):
        planes = pl.ds(2 * h, 2)
        depth[planes] = (least_ref[h] * (1.0 / RADIUS)).T.reshape(2, BY, BZ)
        copies.append(pltpu.make_async_copy(depth.at[planes], depth_hbm.at[planes], sems.at[h]))
        copies[-1].start()
    for copy in copies:
        copy.wait()


def shards(features, conv_weight, mask):
    vmem = pl.BlockSpec(memory_space=pltpu.VMEM)
    hbm = pl.BlockSpec(memory_space=pltpu.HBM)
    tile = (8, BZ)
    dma = pltpu.SemaphoreType.DMA
    out = jax.ShapeDtypeStruct((BX, BY, BZ), F32)
    score, least = pl.pallas_call(
        kernel,
        out_shape=(out, jax.ShapeDtypeStruct((2, 128, BZ), F32)),
        in_specs=[hbm] * 3,
        out_specs=(vmem, vmem),
        scratch_shapes=[
            pltpu.VMEM((32, BX, BY, BZ), jnp.bfloat16),
            pltpu.VMEM((27, 32), jnp.bfloat16),
            pltpu.VMEM((BX, BY, BZ), jnp.int32),
            pltpu.VMEM((288, 512), jnp.bfloat16),
            pltpu.VMEM((3, PLANES, BY + 16, BZ), F32),
            pltpu.VMEM((PLANES, BY + 16, BZ), F32),
            pltpu.VMEM((5, *tile), F32),
            pltpu.VMEM(tile, F32),
            pltpu.VMEM((NI, PLANES, *tile), F32),
            pltpu.VMEM((2, NI, *tile), F32),
            pltpu.VMEM((2, NI, *tile), F32),
            pltpu.VMEM((NI, *tile), F32),
            pltpu.VMEM((NI, 32, BZ), jnp.bfloat16),
            pltpu.VMEM((NI, 32, BZ), jnp.bfloat16),
            pltpu.VMEM((32, *tile), F32),
            pltpu.VMEM((NI, BX, *tile), F32),
            pltpu.VMEM((32, *tile), F32),
            pltpu.VMEM((32, *tile), F32),
            pltpu.VMEM((32, *tile), F32),
            pltpu.VMEM((512, BZ), F32),
            pltpu.VMEM((NJ, BY, BZ), F32),
            pltpu.VMEM((3, NJ, BY, BZ), F32),
            pltpu.VMEM((2, 384, BZ), F32),
            dma((3,)),
        ] + [dma] * 10 + [dma((2,))] * 4 + [dma((3,)), dma((3, 2))],
        compiler_params=pltpu.CompilerParams(
            collective_id=0, has_side_effects=True, vmem_limit_bytes=40 * 1024 * 1024
        ),
    )(*[pltpu.with_memory_space_constraint(x, pltpu.HBM) for x in (features, conv_weight, mask)])
    return pl.pallas_call(
        finish,
        out_shape=(out, out),
        in_specs=[vmem] * 2,
        out_specs=(hbm, hbm),
        scratch_shapes=[pltpu.VMEM((BX, BY, BZ), F32), dma((3,))],
        compiler_params=pltpu.CompilerParams(vmem_limit_bytes=2 * 1024 * 1024),
    )(score, least)


def solution(mesh):
    in_specs = (P(None, "gx", "gy", "gz"), P(), P("gx", "gy", "gz"))
    out_specs = (P("gx", "gy", "gz"), P("gx", "gy", "gz"))
    return jax.shard_map(shards, mesh=mesh, in_specs=in_specs, out_specs=out_specs, check_vma=False)
```
